1024 devices in a mesh: fsdp: 64 (over y_hi, z), seq: 16 (over y_lo, x, core).
Axes of the slice: x: 4, y: 4 (y_hi: 2, y_lo: 2; y = y_hi * 2 + y_lo), z: 32, core: 2. Of those that a mesh axis runs over, the one named last changes fastest.
Arguments:
- clips_in: bfloat16 [64, 16, 384, 320], P('fsdp', 'seq'), may hold values from -81 to 81
- weight_space: bfloat16 [320, 2880], P('fsdp'), may hold values from -0.109375 to 0.109375
- weight_time: bfloat16 [320, 960], P('fsdp'), may hold values from -0.1875 to 0.1875
- norm_gain: float32 [320], replicated, may hold values from 0.1 to 1.9
- norm_shift: float32 [320], replicated, may hold values from -2 to 2
- out_grad: bfloat16 [64, 16, 384, 320], P('fsdp', 'seq'), may hold values from -16 to 16
Outputs:
- mixed: bfloat16 [64, 16, 384, 320], P('fsdp', 'seq')
- in_grad: bfloat16 [64, 16, 384, 320], P('fsdp', 'seq')
- grad_time: float32 [320, 960], P('fsdp')
The draws below stay inside these ranges and needn't reach their ends.
All inputs are finite; a program needn't handle non-finite values.
Results may differ from the reference program's by a relative error of at most 0.015.
Values may be sent and summed in bfloat16 or wider, within the bound.
A program may use at most 32 MiB of HBM per device.

```python
import jax
import jax.numpy as jnp
from jax import lax

CHANNELS = 320
GROUPS = 32
FRAMES = 16
HEIGHT = 16
WIDTH = 24
PIXELS = 384
CLIPS = 64


def draw_clips_in(key, part):
    keys = jax.random.split(key, 3)
    shape = (CLIPS, FRAMES, HEIGHT * WIDTH, CHANNELS)
    frame_pos = jnp.arange(FRAMES).astype(jnp.float32) / (FRAMES - 1)
    pixel_scale = 10.0 ** (jax.random.uniform(keys[1], (CLIPS, 1, HEIGHT * WIDTH, 1), jnp.float32) - 0.5)
    channel_scale = 10.0 ** (jax.random.uniform(keys[2], (1, 1, 1, CHANNELS), jnp.float32) - 0.5)
    base = jnp.clip(jax.random.normal(keys[0], shape, jnp.float32), -4.0, 4.0)
    frame_scale = 2.0 ** (2.0 * frame_pos - 1.0)
    values = base * frame_scale[None, :, None, None] * pixel_scale * channel_scale
    return values.astype(jnp.bfloat16)


def spiked(entries, key, source, target, shards_of, factor):
    owner, partner = [(jnp.arange(entries.shape[axis_at]) // (entries.shape[axis_at] // shards_of)).reshape([-1 if axis == axis_at else 1 for axis in range(entries.ndim)]) for axis_at in (source, target)]
    chosen = jax.random.permutation(key, shards_of)[partner]
    strong = (owner == chosen) | (owner == (partner + shards_of // 2) % shards_of)
    return jnp.where(strong, factor * entries, entries)


def steps_of(rng, extent, pieces, low, largest):
    factor_of = 1.0
    for position, parts in pieces:
        heights = jax.random.uniform(jax.random.fold_in(jax.random.fold_in(rng, 6), position), (parts,), jnp.float32, low / len(pieces), largest / len(pieces))
        factor_of = factor_of * jnp.repeat(jnp.exp(heights), extent[position] // parts).reshape((-1,) + (1,) * (len(extent) - 1 - position))
    return factor_of


def noise(rng, shape, width, most, shards=(), kind=jnp.bfloat16):
    gain = steps_of(rng, shape, shards, -0.22, 0.18) if shards else 1.0
    values = jax.random.normal(rng, shape, jnp.float32) * width * gain
    return jnp.minimum(jnp.maximum(values, -most), most).astype(kind)


def bell_draw_with(rng, shape, scale, bound, pieces, heavy, dtype=jnp.bfloat16):
    result = scale * jax.random.normal(rng, shape, jnp.float32)
    if pieces:
        result = result * steps_of(rng, shape, pieces, -0.22, 0.18)
    return jnp.clip(spiked(result, jax.random.fold_in(rng, 3), *heavy), -bound, bound).astype(dtype)


def setup_inputs(seed: int = 0) -> dict:
    splits = jax.random.split(jax.random.key(seed), 7)
    return {
        "clips_in": draw_clips_in(jax.random.fold_in(splits[6], 71), 0),
        "weight_space": noise(splits[1], (CHANNELS, 9 * CHANNELS), (9 * CHANNELS) ** -0.5, 0.109375, ((0, 64),)),
        "weight_time": noise(splits[2], (CHANNELS, 3 * CHANNELS), (3 * CHANNELS) ** -0.5, 0.1875, ((0, 64),)),
        "norm_gain": jnp.clip(1.0 + 0.18 * jax.random.normal(splits[3], (CHANNELS,), jnp.float32), 0.1, 1.9),
        "norm_shift": noise(splits[4], (CHANNELS,), 0.5, 2.0, (), jnp.float32),
        "out_grad": bell_draw_with(splits[5], (CLIPS, FRAMES, PIXELS, CHANNELS), 1.0, 16.0, ((0, 64), (1, 16)), (0, 3, 64, 4.0)),
    }


EPSILON = 1e-05

def contract_last(left_rows, right_rows):
    return jnp.dot(left_rows, right_rows.T, preferred_element_type=jnp.float32)

def contract_first(left_rows, right_rows):
    return jnp.dot(left_rows.T, right_rows, preferred_element_type=jnp.float32)

def space_shift(frames_in, offset):
    shift_row, shift_col = (offset // 3, offset % 3)
    frame_count, pixels, channels = frames_in.shape
    image_grid = frames_in.reshape(frame_count, HEIGHT, WIDTH, channels)
    padded = jnp.pad(image_grid, ((0, 0), (1, 1), (1, 1), (0, 0)))
    window = padded[:, shift_row:shift_row + HEIGHT, shift_col:shift_col + WIDTH, :]
    return window.reshape(frame_count * pixels, channels)

def space_unshift(flat_rows, frame_count, offset):
    shift_row, shift_col = (offset // 3, offset % 3)
    channels = flat_rows.shape[1]
    image_grid = flat_rows.reshape(frame_count, HEIGHT, WIDTH, channels)
    padded = jnp.pad(image_grid, ((0, 0), (1, 1), (1, 1), (0, 0)))
    window = padded[:, 2 - shift_row:2 - shift_row + HEIGHT, 2 - shift_col:2 - shift_col + WIDTH, :]
    return window.reshape(frame_count * HEIGHT * WIDTH, channels)

def conv_space(frames_in, weight):
    channels = weight.shape[0]
    summed = jnp.zeros((frames_in.shape[0] * frames_in.shape[1], channels), jnp.float32)
    for offset in range(9):
        summed = summed + contract_last(space_shift(frames_in, offset), weight[:, offset * channels:(offset + 1) * channels])
    return summed

def conv_space_back(grad_rows, weight, frame_count):
    channels = weight.shape[0]
    summed = jnp.zeros(grad_rows.shape, jnp.float32)
    for offset in range(9):
        product = jnp.dot(grad_rows, weight[:, offset * channels:(offset + 1) * channels], preferred_element_type=jnp.float32)
        summed = summed + space_unshift(product, frame_count, offset)
    return summed

def pad_frames(values):
    return jnp.pad(values, ((0, 0), (1, 1), (0, 0), (0, 0)))

def conv_time(extended, weight):
    clip_count, frames_ext, pixels, channels = extended.shape
    frame_count = frames_ext - 2
    summed = jnp.zeros((clip_count * frame_count * pixels, channels), jnp.float32)
    for offset in range(3):
        slab_rows = extended[:, offset:offset + frame_count].reshape(-1, channels)
        summed = summed + contract_last(slab_rows, weight[:, offset * channels:(offset + 1) * channels])
    return summed.reshape(clip_count, frame_count, pixels, channels)

def conv_time_back(extended, weight):
    clip_count, frames_ext, pixels, channels = extended.shape
    frame_count = frames_ext - 2
    summed = jnp.zeros((clip_count * frame_count * pixels, channels), jnp.float32)
    for offset in range(3):
        slab_rows = extended[:, 2 - offset:2 - offset + frame_count].reshape(-1, channels)
        summed = summed + jnp.dot(slab_rows, weight[:, offset * channels:(offset + 1) * channels], preferred_element_type=jnp.float32)
    return summed.reshape(clip_count, frame_count, pixels, channels)

def group_mean(totals, counted):
    clip_count, channels = totals.shape
    per_group = channels // GROUPS
    average = totals.reshape(clip_count, GROUPS, per_group).sum(-1) / counted
    return jnp.repeat(average, per_group, axis=1)

def group_stats(first_sums, second_sums, counted):
    average = group_mean(first_sums, counted)
    squares = group_mean(second_sums, counted)
    inv_std = lax.rsqrt(squares - average * average + EPSILON)
    return (average, inv_std)

def reference(clips_in, weight_space, weight_time, norm_gain, norm_shift, out_grad):
    channels = CHANNELS
    counted = FRAMES * PIXELS * (channels // GROUPS)

    def one_clip(carry, inputs):
        clip, grad_clip = inputs
        frames_in = clip
        hidden = conv_space(frames_in, weight_space).reshape(1, FRAMES, PIXELS, channels)
        first_sums = lax.optimization_barrier(jnp.sum(hidden, axis=(1, 2)))
        second_sums = lax.optimization_barrier(jnp.sum(hidden * hidden, axis=(1, 2)))
        average, inv_std = group_stats(first_sums, second_sums, counted)
        normed = (hidden - average[:, None, None, :]) * inv_std[:, None, None, :]
        preact = normed * norm_gain + norm_shift
        activation = jax.nn.silu(preact).astype(jnp.bfloat16)
        act_ext = pad_frames(activation)
        mixed = conv_time(act_ext, weight_time).astype(jnp.bfloat16)
        grad_side = grad_clip[None]
        grad_ext = pad_frames(grad_side)
        act_grad = conv_time_back(grad_ext, weight_time).astype(jnp.bfloat16)
        sigmoid_val = jax.nn.sigmoid(preact)
        slopes = sigmoid_val * (1.0 + preact * (1.0 - sigmoid_val))
        scaled = act_grad.astype(jnp.float32) * slopes * norm_gain
        mean_one = group_mean(lax.optimization_barrier(jnp.sum(scaled, axis=(1, 2))), counted)
        mean_two = group_mean(lax.optimization_barrier(jnp.sum(scaled * normed, axis=(1, 2))), counted)
        hid_grad = (inv_std[:, None, None, :] * (scaled - mean_one[:, None, None, :] - normed * mean_two[:, None, None, :])).astype(jnp.bfloat16)
        grad_rows = hid_grad.reshape(-1, channels)
        in_grad = conv_space_back(grad_rows, weight_space, FRAMES).reshape(FRAMES, PIXELS, channels).astype(jnp.bfloat16)
        time_rows = grad_side.reshape(-1, channels)
        time_term = jnp.concatenate([contract_first(time_rows, act_ext[:, offset:offset + FRAMES].reshape(-1, channels)) for offset in range(3)], axis=1)
        return (carry + time_term, (mixed[0], in_grad))
    start = jnp.zeros((channels, 3 * channels), jnp.float32)
    totals, stacked = lax.scan(one_clip, start, (clips_in, out_grad))
    factor = 1.0 / (CLIPS * FRAMES)
    return (stacked[0], stacked[1], totals * factor)
```

```python
import jax
import jax.numpy as jnp
from jax import lax
from jax.experimental import pallas as pl
from jax.experimental.pallas import tpu as pltpu
from jax.sharding import PartitionSpec as P

GROUPS = 32
FRAMES = 16
HEIGHT = 16
WIDTH = 24
PIXELS = HEIGHT * WIDTH
CH = 320
EPSILON = 1e-05
NZ = 32
NEAR = (-3, -2, -1, 1, 2, 3, 4)
TIME_AT = 3072
COLS = 4096
BLK = 256
MESH = pl.DeviceIdType.MESH
F32 = jnp.float32
BF16 = jnp.bfloat16


def nt(left, right):
    return lax.dot_general(left, right, (((1,), (1,)), ((), ())), preferred_element_type=F32)


def nn(left, right):
    return lax.dot_general(left, right, (((1,), (0,)), ((), ())), preferred_element_type=F32)


def rows_down(values):
    zeros = jnp.zeros((WIDTH, values.shape[1]), values.dtype)
    return jnp.concatenate([zeros, values[: PIXELS - WIDTH]], axis=0)


def rows_up(values):
    zeros = jnp.zeros((WIDTH, values.shape[1]), values.dtype)
    return jnp.concatenate([values[WIDTH:], zeros], axis=0)


def kernel(
    x_ref,
    shard_ref,
    gain_ref,
    shift_ref,
    og_ref,
    mixed_ref,
    ing_ref,
    gt_ref,
    ogr,
    fbuf,
    nbuf,
    wbuf,
    xcol,
    st1,
    st2,
    act_ref,
    actr,
    gsend,
    grecv,
    ysend,
    yrecv,
    n2send,
    n2recv,
    f2send,
    f2recv,
    fin,
    rim_s,
    rim_r,
    far_s,
    far_r,
    near_s,
    near_r,
    p1_s,
    p1_r,
    p2_s,
    p2_r,
    p3_s,
    p3_r,
    st1_s,
    st1_r,
    st2_s,
    st2_r,
    arim_s,
    arim_r,
    ga_s,
    ga_r,
    gy_s,
    gy_r,
    gn_s,
    gn_r,
    gf_s,
    gf_r,
    fin_s,
    fin_r,
):
    f = lax.axis_index("fsdp")
    s = lax.axis_index("seq")
    z = f % NZ
    yh = f // NZ
    c = s % 2
    x = (s // 2) % 4
    yl = s // 8
    y = yh * 2 + yl
    res = z % 8
    oct_ = z // 8

    def copy(src, dst, send, recv, fdev, sdev):
        return pltpu.make_async_remote_copy(
            src_ref=src,
            dst_ref=dst,
            send_sem=send,
            recv_sem=recv,
            device_id=(fdev, sdev),
            device_id_type=MESH,
        )

    def zpeer(d):
        return yh * NZ + (z + d + NZ) % NZ

    barrier = pltpu.get_barrier_semaphore()

    def hello(fdev, sdev):
        pl.semaphore_signal(barrier, inc=1, device_id=(fdev, sdev), device_id_type=MESH)

    for j in range(1, 16):
        hello(f, (s + j) % 16)
    for d in (-4, -3, -2, -1, 1, 2, 3, 4, 8, 16, 24):
        hello(zpeer(d), s)
    other = (f + NZ) % (2 * NZ)
    hello(other, s)
    hello(other, (s + 8) % 16)

    def colblock(xx, yll, cc):
        return (1 - cc) * (4 * yll + xx) + cc * (8 + 2 * xx + yll)

    def wblock(yhh, yll, xx, cc):
        cb = colblock(xx, yll, cc)
        return wbuf.at[
            pl.ds(pl.multiple_of(yhh * 160, 32), 160), pl.ds(pl.multiple_of(cb * BLK, BLK), BLK)
        ]

    mycol = colblock(x, yl, c)
    fbuf[oct_] = shard_ref[:, pl.ds(pl.multiple_of(mycol * BLK, BLK), BLK)]

    pl.semaphore_wait(barrier, 28)

    far = []
    for j in (1, 2, 3):
        cp = copy(fbuf.at[oct_], fbuf.at[oct_], far_s.at[j], far_r.at[j], zpeer(8 * j), s)
        cp.start()
        far.append(cp)
    rim_up = copy(og_ref, ogr.at[0], rim_s.at[0], rim_r.at[0], f, (s + 1) % 16)
    rim_down = copy(og_ref, ogr.at[1], rim_s.at[1], rim_r.at[1], f, (s + 15) % 16)
    rim_up.start()
    rim_down.start()

    def far_in(j):
        src = (oct_ - j + 4) % 4
        return copy(fbuf.at[src], fbuf.at[src], far_s.at[j], far_r.at[j], zpeer(8 * j), s)

    for j in (1, 2, 3):
        far_in(j).wait_recv()
    nbuf[res] = jnp.concatenate([fbuf[m].astype(F32) for m in range(4)], axis=0).astype(BF16)
    near = []
    for n, d in enumerate(NEAR):
        cp = copy(nbuf.at[res], nbuf.at[res], near_s.at[n], near_r.at[n], zpeer(d), s)
        cp.start()
        near.append(cp)

    col = lax.broadcasted_iota(jnp.int32, (HEIGHT, WIDTH, CH), 1).reshape(PIXELS, CH)
    inp = x_ref[...].astype(F32)
    left = jnp.where(col >= 1, pltpu.roll(inp, 1, 0), 0.0)
    right = jnp.where(col <= WIDTH - 2, pltpu.roll(inp, PIXELS - 1, 0), 0.0)
    for b, moved in enumerate((left, inp, right)):
        for a, shifted in enumerate((rows_down(moved), moved, rows_up(moved))):
            at = (3 * a + b) * CH
            xcol[:, at : at + CH] = shifted.astype(BF16)
    xcol[:, 9 * CH :] = jnp.zeros((PIXELS, TIME_AT - 9 * CH), BF16)

    def one_hot(shape, slot_dim):
        slot = lax.broadcasted_iota(jnp.int32, shape, slot_dim)
        row = lax.broadcasted_iota(jnp.int32, shape, 1 - slot_dim)
        within = slot & 7
        target = ((slot >> 5) + (((slot >> 3) & 3) << 3)) * 5 + within
        return jnp.where((target == row) & (within < 5), 1.0, 0.0).astype(BF16)

    for n, d in enumerate(NEAR):
        src = (res - d + 8) % 8
        copy(nbuf.at[src], nbuf.at[src], near_s.at[n], near_r.at[n], zpeer(d), s).wait_recv()
    packed = nn(one_hot((160, 256), 1), nbuf[...].reshape(256, BLK)).astype(BF16)
    wbuf[
        pl.ds(pl.multiple_of(yh * 160, 32), 160), pl.ds(pl.multiple_of(mycol * BLK, BLK), BLK)
    ] = packed

    def dev(yy, xx):
        return (yy // 2) * NZ + z, (yy % 2) * 8 + xx * 2 + c

    def block_of(yy, xx, cc):
        return wblock(yy // 2, yy % 2, xx, cc)

    mine = block_of(y, x, c)
    sib = s + 1 - 2 * c

    def to_sibling(ref, n):
        copy(ref, ref, p3_s.at[n], p3_r.at[n], f, sib).start()

    for j in range(1, 4):
        fd, sd = dev((y + c * j) % 4, (x + (1 - c) * j) % 4)
        copy(mine, mine, p1_s.at[j], p1_r.at[j], fd, sd).start()

    def first_block(i):
        return (y - c * i + 4) % 4, (x - (1 - c) * i + 4) % 4

    for i in range(4):
        by, bx = first_block(i)
        ref = block_of(by, bx, c)
        if i:
            copy(ref, ref, p1_s.at[i], p1_r.at[i], f, sib).wait_recv()
        for j in range(1, 4):
            fd, sd = dev((y + (1 - c) * j) % 4, (x + c * j) % 4)
            copy(ref, ref, p2_s.at[4 * j + i], p2_r.at[4 * j + i], fd, sd).start()
        to_sibling(ref, i)

    def second_block(i, j, cc):
        return (
            (y - (1 - cc) * j - cc * i + 8) % 4,
            (x - cc * j - (1 - cc) * i + 8) % 4,
        )

    for j in range(1, 4):
        for i in range(4):
            by, bx = second_block(i, j, c)
            ref = block_of(by, bx, c)
            copy(ref, ref, p2_s.at[4 * j + i], p2_r.at[4 * j + i], f, sib).wait_recv()
            to_sibling(ref, 4 * j + i)
    for n in range(16):
        by, bx = second_block(n % 4, n // 4, 1 - c)
        ref = block_of(by, bx, 1 - c)
        copy(ref, ref, p3_s.at[n], p3_r.at[n], f, sib).wait_recv()

    hidden = nt(xcol[...], wbuf[:, 0:TIME_AT])
    sums = jnp.concatenate(
        [jnp.sum(hidden, axis=0, keepdims=True), jnp.sum(hidden * hidden, axis=0, keepdims=True)],
        axis=0,
    )

    def exchange(buf, value, send, recv):
        buf[s] = value

        def go(j, carry):
            copy(buf.at[s], buf.at[s], send.at[j], recv.at[j], f, (s + j) % 16).start()
            return carry

        lax.fori_loop(1, 16, go, 0)

    def arrived(buf, send, recv):
        def take(j, carry):
            src = (s - j + 16) % 16
            copy(buf.at[src], buf.at[src], send.at[j], recv.at[j], f, src).wait_recv()
            return carry

        lax.fori_loop(1, 16, take, 0)

    exchange(st1, sums, st1_s, st1_r)

    has_left = jnp.where(s > 0, 1.0, 0.0)
    has_right = jnp.where(s < FRAMES - 1, 1.0, 0.0)
    rim_up.wait_recv()
    rim_down.wait_recv()
    wtime = wbuf[:, TIME_AT:COLS]
    taps = [wtime[:, k * CH : (k + 1) * CH] for k in range(3)]
    act_grad = (
        (nn(ogr[1], taps[0]) * has_right + nn(og_ref[...], taps[1]) + nn(ogr[0], taps[2]) * has_left)
        .astype(BF16)
        .astype(F32)
    )
    og_t = [v.T for v in (ogr[1], og_ref[...], ogr[0])]

    row_i = lax.broadcasted_iota(jnp.int32, (CH, CH), 0)
    col_i = lax.broadcasted_iota(jnp.int32, (CH, CH), 1)
    per = CH // GROUPS
    low = row_i - (row_i % per)
    same = jnp.where((col_i >= low) & (col_i < low + per), 1.0, 0.0)
    counted = float(FRAMES * PIXELS * per)

    def group_means(buf):
        total = jnp.sum(buf[...], axis=0)
        grouped = lax.dot_general(
            total,
            same,
            (((1,), (0,)), ((), ())),
            precision=lax.Precision.HIGHEST,
            preferred_element_type=F32,
        )
        return grouped[0:1] / counted, grouped[1:2] / counted

    arrived(st1, st1_s, st1_r)
    average, squares = group_means(st1)
    inv_std = lax.rsqrt(squares - average * average + EPSILON)
    gain = gain_ref[...]
    normed = (hidden - average) * inv_std
    preact = normed * gain + shift_ref[...]
    sig = 1.0 / (1.0 + jnp.exp(-preact))
    activation = (preact * sig).astype(BF16)
    act_ref[...] = activation

    for k, weight in enumerate((has_right, None, has_left)):
        part = nn(og_t[k], activation)
        if weight is not None:
            part = part * weight
        for b in range(5):
            at = 64 * b
            gsend[5 * k + b] = jnp.concatenate(
                [part[0:160, at : at + 64], part[160:320, at : at + 64]], axis=1
            ).astype(BF16)
    gsend[15] = jnp.zeros((160, 128), BF16)

    def ga_go(j, carry):
        peer = (s + j) % 16
        copy(gsend.at[peer], grecv.at[s], ga_s.at[j], ga_r.at[j], f, peer).start()
        return carry

    lax.fori_loop(1, 16, ga_go, 0)
    grecv[s] = gsend[s]
    arim_up = copy(act_ref, actr.at[0], arim_s.at[0], arim_r.at[0], f, (s + 1) % 16)
    arim_down = copy(act_ref, actr.at[1], arim_s.at[1], arim_r.at[1], f, (s + 15) % 16)
    arim_up.start()
    arim_down.start()

    scaled = act_grad * (sig * (1.0 + preact * (1.0 - sig))) * gain
    back = jnp.concatenate(
        [jnp.sum(scaled, axis=0, keepdims=True), jnp.sum(scaled * normed, axis=0, keepdims=True)],
        axis=0,
    )
    exchange(st2, back, st2_s, st2_r)

    arim_up.wait_recv()
    arim_down.wait_recv()
    mixed_ref[...] = (
        nt(actr[0], taps[0]) * has_left + nt(activation, taps[1]) + nt(actr[1], taps[2]) * has_right
    ).astype(BF16)

    arrived(st2, st2_s, st2_r)
    mean_one, mean_two = group_means(st2)
    hid_grad = (inv_std * (scaled - mean_one - normed * mean_two)).astype(BF16)

    def spread(b):
        parts = [nn(hid_grad, wbuf[:, 0:TIME_AT][:, (3 * a + b) * CH : (3 * a + b + 1) * CH]) for a in range(3)]
        return rows_up(parts[0]) + parts[1] + rows_down(parts[2])

    total = spread(1)
    total = total + jnp.where(col <= WIDTH - 2, pltpu.roll(spread(0), PIXELS - 1, 0), 0.0)
    total = total + jnp.where(col >= 1, pltpu.roll(spread(2), 1, 0), 0.0)
    ing_ref[...] = total.astype(BF16)

    def ga_take(j, carry):
        src = (s - j + 16) % 16
        copy(gsend.at[src], grecv.at[src], ga_s.at[j], ga_r.at[j], f, src).wait_recv()
        return carry

    lax.fori_loop(1, 16, ga_take, 0)
    share = jnp.zeros((160, 128), F32)
    for i in range(16):
        share = share + grecv[i].astype(F32)
    ysend[...] = share.astype(BF16)
    ycopy = copy(ysend, yrecv, gy_s.at[0], gy_r.at[0], other, s)
    ycopy.start()
    ycopy.wait_recv()
    share = share + yrecv[...].astype(F32)
    is_hi = yh.astype(F32)
    share = share * (1.0 - is_hi) + pltpu.roll(share, 64, 1) * is_hi
    n2send[...] = nn(one_hot((256, 160), 0), share.astype(BF16)).astype(BF16).reshape(8, 32, 128)
    for n, d in enumerate(NEAR):
        to = (res + d + 8) % 8
        copy(n2send.at[to], n2recv.at[n], gn_s.at[n], gn_r.at[n], zpeer(d), s).start()
    near_sum = n2send[res].astype(F32)
    for n, d in enumerate(NEAR):
        copy(n2send.at[res], n2recv.at[n], gn_s.at[n], gn_r.at[n], zpeer(d), s).wait_recv()
        near_sum = near_sum + n2recv[n].astype(F32)
    f2send[...] = near_sum.reshape(4, 8, 128)
    for j in (1, 2, 3):
        to = (oct_ + j) % 4
        copy(f2send.at[to], f2recv.at[j], gf_s.at[j], gf_r.at[j], zpeer(8 * j), s).start()
    last = f2send[oct_]
    for j in (1, 2, 3):
        copy(f2send.at[oct_], f2recv.at[j], gf_s.at[j], gf_r.at[j], zpeer(8 * j), s).wait_recv()
        last = last + f2recv[j]
    clips = lax.axis_size("fsdp")
    exchange(fin, last * (1.0 / (clips * FRAMES)), fin_s, fin_r)
    arrived(fin, fin_s, fin_r)
    gt_ref[...] = jnp.concatenate([fin[b][:, 0:64] for b in range(15)], axis=1)[0:5]

    for cp in far + near + [rim_up, rim_down, arim_up, arim_down, ycopy]:
        cp.wait_send()
    for j in range(1, 4):
        copy(mine, mine, p1_s.at[j], p1_r.at[j], f, sib).wait_send()
        for i in range(4):
            by, bx = first_block(i)
            ref = block_of(by, bx, c)
            copy(ref, ref, p2_s.at[4 * j + i], p2_r.at[4 * j + i], f, sib).wait_send()
    for n in range(16):
        by, bx = second_block(n % 4, n // 4, c)
        ref = block_of(by, bx, c)
        copy(ref, ref, p3_s.at[n], p3_r.at[n], f, sib).wait_send()

    def sent(j, carry):
        peer = (s + j) % 16
        copy(st1.at[s], st1.at[s], st1_s.at[j], st1_r.at[j], f, peer).wait_send()
        copy(st2.at[s], st2.at[s], st2_s.at[j], st2_r.at[j], f, peer).wait_send()
        copy(gsend.at[peer], grecv.at[s], ga_s.at[j], ga_r.at[j], f, peer).wait_send()
        copy(fin.at[s], fin.at[s], fin_s.at[j], fin_r.at[j], f, peer).wait_send()
        return carry

    lax.fori_loop(1, 16, sent, 0)
    for n, d in enumerate(NEAR):
        to = (res + d + 8) % 8
        copy(n2send.at[to], n2recv.at[n], gn_s.at[n], gn_r.at[n], zpeer(d), s).wait_send()
    for j in (1, 2, 3):
        to = (oct_ + j) % 4
        copy(f2send.at[to], f2recv.at[j], gf_s.at[j], gf_r.at[j], zpeer(8 * j), s).wait_send()


def local(clips_in, weight_space, weight_time, norm_gain, norm_shift, out_grad):
    shard = jnp.concatenate(
        [
            jnp.pad(weight_space, ((0, 3), (0, TIME_AT - 9 * CH))),
            jnp.pad(weight_time, ((0, 3), (0, COLS - TIME_AT - 3 * CH))),
        ],
        axis=1,
    )
    vmem = pl.BlockSpec(memory_space=pltpu.VMEM)
    dma = pltpu.SemaphoreType.DMA
    mixed, in_grad, grad_time = pl.pallas_call(
        kernel,
        out_shape=(
            jax.ShapeDtypeStruct((PIXELS, CH), BF16),
            jax.ShapeDtypeStruct((PIXELS, CH), BF16),
            jax.ShapeDtypeStruct((5, 3 * CH), F32),
        ),
        in_specs=[vmem] * 5,
        out_specs=(vmem, vmem, vmem),
        scratch_shapes=[
            pltpu.VMEM((2, PIXELS, CH), BF16),
            pltpu.VMEM((4, 8, BLK), BF16),
            pltpu.VMEM((8, 32, BLK), BF16),
            pltpu.VMEM((CH, COLS), BF16),
            pltpu.VMEM((PIXELS, TIME_AT), BF16),
            pltpu.VMEM((16, 2, CH), F32),
            pltpu.VMEM((16, 2, CH), F32),
            pltpu.VMEM((PIXELS, CH), BF16),
            pltpu.VMEM((2, PIXELS, CH), BF16),
            pltpu.VMEM((16, 160, 128), BF16),
            pltpu.VMEM((16, 160, 128), BF16),
            pltpu.VMEM((160, 128), BF16),
            pltpu.VMEM((160, 128), BF16),
            pltpu.VMEM((8, 32, 128), BF16),
            pltpu.VMEM((7, 32, 128), BF16),
            pltpu.VMEM((4, 8, 128), F32),
            pltpu.VMEM((4, 8, 128), F32),
            pltpu.VMEM((16, 8, 128), F32),
        ]
        + [dma((n,)) for n in (2, 2, 4, 4, 7, 7, 4, 4, 16, 16, 16, 16)]
        + [dma((16,))] * 4
        + [dma((2,))] * 2
        + [dma((16,))] * 2
        + [dma((1,))] * 2
        + [dma((7,))] * 2
        + [dma((4,))] * 2
        + [dma((16,))] * 2,
        compiler_params=pltpu.CompilerParams(
            collective_id=0, has_side_effects=True, vmem_limit_bytes=56 * 1024 * 1024
        ),
    )(
        clips_in.reshape(PIXELS, CH),
        shard,
        norm_gain.reshape(1, CH),
        norm_shift.reshape(1, CH),
        out_grad.reshape(PIXELS, CH),
    )
    return mixed.reshape(clips_in.shape), in_grad.reshape(clips_in.shape), grad_time


def solution(mesh):
    in_specs = (
        P("fsdp", "seq", None, None),
        P("fsdp", None),
        P("fsdp", None),
        P(),
        P(),
        P("fsdp", "seq", None, None),
    )
    out_specs = (P("fsdp", "seq", None, None), P("fsdp", "seq", None, None), P("fsdp", None))
    return jax.shard_map(local, mesh=mesh, in_specs=in_specs, out_specs=out_specs, check_vma=False)
```

```python
import jax
import jax.numpy as jnp
from jax import lax
from jax.experimental import pallas as pl
from jax.experimental.pallas import tpu as pltpu
from jax.sharding import PartitionSpec as P

GROUPS = 32
FRAMES = 16
HEIGHT = 16
WIDTH = 24
PIXELS = HEIGHT * WIDTH
CH = 320
EPSILON = 1e-05
NZ = 32
TIME_AT = 3072
COLS = 4096
BLK = 256
MESH = pl.DeviceIdType.MESH
F32 = jnp.float32
BF16 = jnp.bfloat16


def nt(left, right):
    return lax.dot_general(left, right, (((1,), (1,)), ((), ())), preferred_element_type=F32)


def nn(left, right):
    return lax.dot_general(left, right, (((1,), (0,)), ((), ())), preferred_element_type=F32)


def flight_order(i):
    half = (i + 1) // 2
    return 16 + half * (1 - 2 * (i % 2))


def kernel(
    x_ref,
    ws_ref,
    wt_ref,
    gain_ref,
    shift_ref,
    og_ref,
    mixed_ref,
    ing_ref,
    gt_ref,
    ogr,
    wpad,
    zbuf,
    wbuf,
    xcol,
    st1,
    st2,
    act_ref,
    actr,
    gall,
    gsib,
    gchip,
    gplane,
    zsend,
    zrecv,
    fval,
    fin,
    wtrans,
    rim_s,
    rim_r,
    zw_s,
    zw_r,
    p1_s,
    p1_r,
    p2_s,
    p2_r,
    p3_s,
    p3_r,
    st1_s,
    st1_r,
    st2_s,
    st2_r,
    arim_s,
    arim_r,
    gc_s,
    gc_r,
    gp_s,
    gp_r,
    gz_s,
    gz_r,
    fin_s,
    fin_r,
):
    f = lax.axis_index("fsdp")
    s = lax.axis_index("seq")
    z = f % NZ
    yh = f // NZ
    c = s % 2
    x = (s // 2) % 4
    yl = s // 8
    y = yh * 2 + yl
    chip = y * 4 + x
    sib = s + 1 - 2 * c
    pending = []

    def copy(src, dst, send, recv, fdev, sdev):
        return pltpu.make_async_remote_copy(
            src_ref=src,
            dst_ref=dst,
            send_sem=send,
            recv_sem=recv,
            device_id=(fdev, sdev),
            device_id_type=MESH,
        )

    def start(cp):
        cp.start()
        pending.append(cp.wait_send)

    def loop(low, high, body):
        def step(i, carry):
            body(i)
            return carry

        lax.fori_loop(low, high, step, 0)

    def zpeer(d):
        return yh * NZ + (z + d) % NZ

    def on_chip(q, cc):
        return (q // 8) * NZ + z, ((q // 4) % 2) * 8 + (q % 4) * 2 + cc

    barrier = pltpu.get_barrier_semaphore()

    def hello(fdev, sdev):
        pl.semaphore_signal(barrier, inc=1, device_id=(fdev, sdev), device_id_type=MESH)

    loop(0, 31, lambda i: hello(zpeer(flight_order(i)), s))

    def hello_plane(j):
        q = (chip + j) % 16
        for cc in (0, 1):
            fd, sd = on_chip(q, cc)
            hello(fd, sd)

    loop(1, 16, hello_plane)
    hello(f, sib)

    def colblock(xx, yll, cc):
        return (1 - cc) * (4 * yll + xx) + cc * (8 + 2 * xx + yll)

    def wblock(yy, xx, cc):
        cb = colblock(xx, yy % 2, cc)
        return wbuf.at[
            pl.ds(pl.multiple_of((yy // 2) * 160, 32), 160),
            pl.ds(pl.multiple_of(cb * BLK, BLK), BLK),
        ]

    mycol = pl.multiple_of(colblock(x, yl, c) * BLK, BLK)
    wpad[...] = jnp.zeros((8, COLS), F32)
    wpad[0:5, 0 : 9 * CH] = ws_ref[...].astype(F32)
    wpad[0:5, TIME_AT : TIME_AT + 3 * CH] = wt_ref[...].astype(F32)
    zbuf[z] = wpad[:, pl.ds(mycol, BLK)].astype(BF16)

    pix = lax.broadcasted_iota(jnp.int32, (1, PIXELS), 1)
    col = pix - WIDTH * ((pix * 2731) >> 16)

    def inside(a, b):
        ok = pix >= 0
        if a == 0:
            ok = ok & (pix >= WIDTH)
        if a == 2:
            ok = ok & (pix < PIXELS - WIDTH)
        if b == 0:
            ok = ok & (col >= 1)
        if b == 2:
            ok = ok & (col <= WIDTH - 2)
        return ok

    def moved(values, a, b):
        step = WIDTH * (a - 1) + b - 1
        if step == 0:
            return values
        return jnp.where(inside(a, b), pltpu.roll(values, (-step) % PIXELS, 1), 0.0)

    inp = x_ref[...].astype(F32)
    for a in range(3):
        for b in range(3):
            at = (3 * a + b) * CH
            xcol[at : at + CH, :] = moved(inp, a, b).astype(BF16)
    xcol[9 * CH :, :] = jnp.zeros((TIME_AT - 9 * CH, PIXELS), BF16)

    pl.semaphore_wait(barrier, 62)

    def zw_copy(d, slot):
        return copy(zbuf.at[slot], zbuf.at[slot], zw_s.at[d], zw_r.at[d], zpeer(d), s)

    loop(0, 31, lambda i: zw_copy(flight_order(i), z).start())
    pending.append(lambda: loop(1, 32, lambda d: zw_copy(d, z).wait_send()))
    rim_up = copy(og_ref, ogr.at[0], rim_s.at[0], rim_r.at[0], f, (s + 1) % 16)
    rim_down = copy(og_ref, ogr.at[1], rim_s.at[1], rim_r.at[1], f, (s + 15) % 16)
    start(rim_up)
    start(rim_down)
    loop(1, 32, lambda d: zw_copy(d, (z - d + NZ) % NZ).wait_recv())

    slot = lax.broadcasted_iota(jnp.int32, (160, 256), 1)
    row = lax.broadcasted_iota(jnp.int32, (160, 256), 0)
    pick = jnp.where(((slot >> 3) * 5 + (slot & 7) == row) & ((slot & 7) < 5), 1.0, 0.0).astype(BF16)
    pieces = zbuf[...].astype(F32).reshape(256, BLK).astype(BF16)
    wbuf[pl.ds(pl.multiple_of(yh * 160, 32), 160), pl.ds(mycol, BLK)] = nn(pick, pieces).astype(BF16)

    def to_sibling(ref, n):
        start(copy(ref, ref, p3_s.at[n], p3_r.at[n], f, sib))

    def first_block(i):
        return (y - c * i + 4) % 4, (x - (1 - c) * i + 4) % 4

    def second_block(i, j, cc):
        return (y - (1 - cc) * j - cc * i + 8) % 4, (x - cc * j - (1 - cc) * i + 8) % 4

    mine = wblock(y, x, c)
    for j in range(1, 4):
        fd, sd = on_chip(((y + c * j) % 4) * 4 + (x + (1 - c) * j) % 4, c)
        start(copy(mine, mine, p1_s.at[j], p1_r.at[j], fd, sd))
    for i in range(4):
        by, bx = first_block(i)
        ref = wblock(by, bx, c)
        if i:
            copy(ref, ref, p1_s.at[i], p1_r.at[i], f, sib).wait_recv()
        for j in range(1, 4):
            fd, sd = on_chip(((y + (1 - c) * j) % 4) * 4 + (x + c * j) % 4, c)
            start(copy(ref, ref, p2_s.at[4 * j + i], p2_r.at[4 * j + i], fd, sd))
        to_sibling(ref, i)
    for i in range(4):
        for j in range(1, 4):
            by, bx = second_block(i, j, c)
            ref = wblock(by, bx, c)
            copy(ref, ref, p2_s.at[4 * j + i], p2_r.at[4 * j + i], f, sib).wait_recv()
            to_sibling(ref, 4 * j + i)
    for n in range(16):
        by, bx = second_block(n % 4, n // 4, 1 - c)
        ref = wblock(by, bx, 1 - c)
        copy(ref, ref, p3_s.at[n], p3_r.at[n], f, sib).wait_recv()

    def lane_sums(values):
        part = values[:, 0:128] + values[:, 128:256] + values[:, 256:384]
        return jnp.sum(part.T, axis=0, keepdims=True)

    def sums_of(first, second):
        return jnp.concatenate([lane_sums(first), lane_sums(second)], axis=0)

    def exchange(buf, value, send, recv):
        buf[s] = value

        def go(j):
            return copy(buf.at[s], buf.at[s], send.at[j], recv.at[j], f, (s + j) % 16)

        loop(1, 16, lambda j: go(j).start())
        pending.append(lambda: loop(1, 16, lambda j: go(j).wait_send()))

    def arrived(buf, send, recv):
        def take(j):
            src = (s - j + 16) % 16
            copy(buf.at[src], buf.at[src], send.at[j], recv.at[j], f, src).wait_recv()

        loop(1, 16, take)

    hidden = nn(wbuf[:, 0:TIME_AT], xcol[...])
    exchange(st1, sums_of(hidden, hidden * hidden), st1_s, st1_r)

    has_left = jnp.where(s > 0, 1.0, 0.0)
    has_right = jnp.where(s < FRAMES - 1, 1.0, 0.0)
    rim_up.wait_recv()
    rim_down.wait_recv()
    wtime = wbuf[:, TIME_AT:COLS]
    taps = [wtime[:, k * CH : (k + 1) * CH] for k in range(3)]
    grads = (ogr[1], og_ref[...], ogr[0])
    act_grad = (
        (
            nn(taps[0].T, grads[0]) * has_right
            + nn(taps[1].T, grads[1])
            + nn(taps[2].T, grads[2]) * has_left
        )
        .astype(BF16)
        .astype(F32)
    )
    per = CH // GROUPS
    row_i = lax.broadcasted_iota(jnp.int32, (CH, CH), 0)
    col_i = lax.broadcasted_iota(jnp.int32, (CH, CH), 1)
    low = row_i - (row_i % per)
    same = jnp.where((col_i >= low) & (col_i < low + per), 1.0, 0.0)
    counted = float(FRAMES * PIXELS * per)

    def group_means(buf):
        grouped = lax.dot_general(
            same,
            jnp.sum(buf[...], axis=0),
            (((1,), (1,)), ((), ())),
            precision=lax.Precision.HIGHEST,
            preferred_element_type=F32,
        )
        return grouped[:, 0:1] / counted, grouped[:, 1:2] / counted

    def column(ref):
        return jnp.broadcast_to(ref[...].reshape(1, CH), (8, CH)).T[:, 0:1]

    gain = column(gain_ref)
    shift = column(shift_ref)

    arrived(st1, st1_s, st1_r)
    average, squares = group_means(st1)
    inv_std = lax.rsqrt(squares - average * average + EPSILON)
    normed = (hidden - average) * inv_std
    preact = normed * gain + shift
    sig = 1.0 / (1.0 + jnp.exp(-preact))
    activation = (preact * sig).astype(BF16)
    act_ref[...] = activation

    for k, weight in enumerate((has_right, None, has_left)):
        part = nt(grads[k], activation)
        if weight is not None:
            part = part * weight
        part = part.astype(BF16)
        for half in range(2):
            for b in range(5):
                at = 64 * b
                gall[half, 5 * k + b] = jnp.concatenate(
                    [
                        part[160 * half : 160 * half + 80, at : at + 64],
                        part[160 * half + 80 : 160 * half + 160, at : at + 64],
                    ],
                    axis=1,
                )
    for half in range(2):
        gall[half, 15] = jnp.zeros((80, 128), BF16)
    core_copy = copy(gall.at[1 - c], gsib, gc_s.at[0], gc_r.at[0], f, sib)
    start(core_copy)

    scaled = act_grad * (sig * (1.0 + preact * (1.0 - sig))) * gain
    exchange(st2, sums_of(scaled, scaled * normed), st2_s, st2_r)

    core_copy.wait_recv()
    gchip[...] = (gall[c].astype(F32) + gsib[...].astype(F32)).astype(BF16)

    def gp_copy(j, to, src):
        fd, sd = on_chip(to, c)
        return copy(gchip.at[to], gplane.at[src], gp_s.at[j], gp_r.at[j], fd, sd)

    loop(1, 16, lambda j: gp_copy(j, (chip + j) % 16, chip).start())
    pending.append(lambda: loop(1, 16, lambda j: gp_copy(j, (chip + j) % 16, chip).wait_send()))
    gplane[chip] = gchip[chip]
    arim_up = copy(act_ref, actr.at[0], arim_s.at[0], arim_r.at[0], f, (s + 1) % 16)
    arim_down = copy(act_ref, actr.at[1], arim_s.at[1], arim_r.at[1], f, (s + 15) % 16)
    start(arim_up)
    start(arim_down)

    arrived(st2, st2_s, st2_r)
    mean_one, mean_two = group_means(st2)
    hid_grad = (inv_std * (scaled - mean_one - normed * mean_two)).astype(BF16)

    def gp_take(j):
        src = (chip - j + 16) % 16
        gp_copy(j, src, src).wait_recv()

    loop(1, 16, gp_take)
    share = jnp.zeros((80, 128), F32)
    for i in range(16):
        share = share + gplane[i].astype(F32)

    slot = lax.broadcasted_iota(jnp.int32, (128, 80), 0)
    row = lax.broadcasted_iota(jnp.int32, (128, 80), 1)
    put = jnp.where(((slot >> 3) * 5 + (slot & 7) == row) & ((slot & 7) < 5), 1.0, 0.0).astype(BF16)
    zsend[...] = nn(put, share.astype(BF16)).reshape(16, 8, 128).astype(BF16)

    def gz_copy(d):
        return copy(zsend.at[(z + d) % 16], zrecv.at[d], gz_s.at[d], gz_r.at[d], zpeer(d), s)

    loop(0, 31, lambda i: gz_copy(flight_order(i)).start())
    pending.append(lambda: loop(1, 32, lambda d: gz_copy(d).wait_send()))
    zrecv[0] = zsend[z % 16]

    wtrans[...] = wbuf[:, 0:TIME_AT].T
    total = nn(wtrans[4 * CH : 5 * CH, :], hid_grad)
    for a in range(3):
        for b in range(3):
            if a != 1 or b != 1:
                at = (3 * a + b) * CH
                total = total + moved(nn(wtrans[at : at + CH, :], hid_grad), 2 - a, 2 - b)
    ing_ref[...] = total.astype(BF16)
    arim_up.wait_recv()
    arim_down.wait_recv()
    mixed_ref[...] = (
        nn(taps[0], actr[0]) * has_left + nn(taps[1], act_ref[...]) + nn(taps[2], actr[1]) * has_right
    ).astype(BF16)

    loop(1, 32, lambda d: gz_copy(d).wait_recv())
    last = jnp.sum(zrecv[...].astype(F32), axis=0)
    right = jnp.where(z >= 16, 1.0, 0.0)
    last = last * (1.0 - right) + pltpu.roll(last, 64, 1) * right
    fval[...] = last * (1.0 / (lax.axis_size("fsdp") * FRAMES))

    def fin_copy(j, src):
        return copy(fval, fin.at[src], fin_s.at[j], fin_r.at[src], c * NZ + z, (s + j) % 16)

    @pl.when(yh == c)
    def _():
        fin[chip] = fval[...]

    @pl.when(yh != c)
    def _():
        fin_copy(0, chip).start()

    loop(1, 16, lambda j: fin_copy(j, chip).start())

    def fin_take(src):
        @pl.when((yh != c) | (src != chip))
        def _():
            fin_copy(0, src).wait_recv()

    loop(0, 16, fin_take)
    gt_ref[...] = jnp.concatenate([fin[b][:, 0:64] for b in range(15)], axis=1)[0:5]

    @pl.when(yh != c)
    def _():
        fin_copy(0, chip).wait_send()

    loop(1, 16, lambda j: fin_copy(j, chip).wait_send())
    for left_over in pending:
        left_over()


def local(clips_in, weight_space, weight_time, norm_gain, norm_shift, out_grad):
    vmem = pl.BlockSpec(memory_space=pltpu.VMEM)
    dma = pltpu.SemaphoreType.DMA
    mixed, in_grad, grad_time = pl.pallas_call(
        kernel,
        out_shape=(
            jax.ShapeDtypeStruct((CH, PIXELS), BF16),
            jax.ShapeDtypeStruct((CH, PIXELS), BF16),
            jax.ShapeDtypeStruct((5, 3 * CH), F32),
        ),
        in_specs=[vmem] * 6,
        out_specs=(vmem, vmem, vmem),
        scratch_shapes=[
            pltpu.VMEM((2, CH, PIXELS), BF16),
            pltpu.VMEM((8, COLS), F32),
            pltpu.VMEM((NZ, 8, BLK), BF16),
            pltpu.VMEM((CH, COLS), BF16),
            pltpu.VMEM((TIME_AT, PIXELS), BF16),
            pltpu.VMEM((16, 2, CH), F32),
            pltpu.VMEM((16, 2, CH), F32),
            pltpu.VMEM((CH, PIXELS), BF16),
            pltpu.VMEM((2, CH, PIXELS), BF16),
            pltpu.VMEM((2, 16, 80, 128), BF16),
            pltpu.VMEM((16, 80, 128), BF16),
            pltpu.VMEM((16, 80, 128), BF16),
            pltpu.VMEM((16, 80, 128), BF16),
            pltpu.VMEM((16, 8, 128), BF16),
            pltpu.VMEM((NZ, 8, 128), BF16),
            pltpu.VMEM((8, 128), F32),
            pltpu.VMEM((16, 8, 128), F32),
            pltpu.VMEM((TIME_AT, CH), BF16),
        ]
        + [dma((n,)) for n in (2, 2, NZ, NZ, 4, 4)]
        + [dma((16,))] * 8
        + [dma((2,))] * 2
        + [dma((1,))] * 2
        + [dma((16,))] * 2
        + [dma((NZ,))] * 2
        + [dma((16,))] * 2,
        compiler_params=pltpu.CompilerParams(
            collective_id=0, has_side_effects=True, vmem_limit_bytes=56 * 1024 * 1024
        ),
    )(
        clips_in.reshape(PIXELS, CH).T,
        weight_space,
        weight_time,
        norm_gain,
        norm_shift,
        out_grad.reshape(PIXELS, CH).T,
    )
    return mixed.T.reshape(clips_in.shape), in_grad.T.reshape(clips_in.shape), grad_time


def solution(mesh):
    in_specs = (
        P("fsdp", "seq", None, None),
        P("fsdp", None),
        P("fsdp", None),
        P(),
        P(),
        P("fsdp", "seq", None, None),
    )
    out_specs = (P("fsdp", "seq", None, None), P("fsdp", "seq", None, None), P("fsdp", None))
    return jax.shard_map(local, mesh=mesh, in_specs=in_specs, out_specs=out_specs, check_vma=False)
```

```python
import jax
import jax.numpy as jnp
from jax import lax
from jax.experimental import pallas as pl
from jax.experimental.pallas import tpu as pltpu
from jax.sharding import PartitionSpec as P

GROUPS = 32
FRAMES = 16
HEIGHT = 16
WIDTH = 24
PIXELS = HEIGHT * WIDTH
CH = 320
EPSILON = 1e-05
NZ = 32
TIME_AT = 3072
COLS = 4096
BLK = 256
MESH = pl.DeviceIdType.MESH
F32 = jnp.float32
BF16 = jnp.bfloat16


def nt(left, right):
    return lax.dot_general(left, right, (((1,), (1,)), ((), ())), preferred_element_type=F32)


def nn(left, right):
    return lax.dot_general(left, right, (((1,), (0,)), ((), ())), preferred_element_type=F32)


def flight_order(i):
    half = (i + 1) // 2
    return 16 + half * (1 - 2 * (i % 2))


def kernel(
    x_hbm,
    ws_hbm,
    wt_hbm,
    gain_ref,
    shift_ref,
    og_hbm,
    mixed_hbm,
    ing_hbm,
    gt_hbm,
    x_ref,
    ws_ref,
    wt_ref,
    og_ref,
    mixed_ref,
    ing_ref,
    gt_ref,
    ogr,
    wpad,
    zbuf,
    wbuf,
    xcol,
    st1,
    st2,
    act_ref,
    actr,
    gout,
    gsib,
    gchip,
    gplane,
    zsend,
    zrecv,
    fval,
    fin,
    wtrans,
    rim_s,
    rim_r,
    zw_s,
    zw_r,
    p1_s,
    p1_r,
    p2_s,
    p2_r,
    p3_s,
    p3_r,
    st1_s,
    st1_r,
    st2_s,
    st2_r,
    arim_s,
    arim_r,
    gc_s,
    gc_r,
    gp_s,
    gp_r,
    gz_s,
    gz_r,
    fin_s,
    fin_r,
    in_sem,
    out_sem,
):
    f = lax.axis_index("fsdp")
    s = lax.axis_index("seq")
    z = f % NZ
    yh = f // NZ
    c = s % 2
    x = (s // 2) % 4
    yl = s // 8
    y = yh * 2 + yl
    chip = y * 4 + x
    sib = s + 1 - 2 * c
    pending = []

    loads = [
        pltpu.make_async_copy(src, dst, in_sem.at[n])
        for n, (src, dst) in enumerate(
            ((ws_hbm, ws_ref), (wt_hbm, wt_ref), (x_hbm, x_ref), (og_hbm, og_ref))
        )
    ]
    for load in loads:
        load.start()

    def copy(src, dst, send, recv, fdev, sdev):
        return pltpu.make_async_remote_copy(
            src_ref=src,
            dst_ref=dst,
            send_sem=send,
            recv_sem=recv,
            device_id=(fdev, sdev),
            device_id_type=MESH,
        )

    def start(cp):
        cp.start()
        pending.append(cp.wait_send)

    def loop(low, high, body):
        def step(i, carry):
            body(i)
            return carry

        lax.fori_loop(low, high, step, 0)

    def zpeer(d):
        return yh * NZ + (z + d) % NZ

    def on_chip(q, cc):
        return (q // 8) * NZ + z, ((q // 4) % 2) * 8 + (q % 4) * 2 + cc

    barrier = pltpu.get_barrier_semaphore()

    def hello(fdev, sdev):
        pl.semaphore_signal(barrier, inc=1, device_id=(fdev, sdev), device_id_type=MESH)

    loop(0, 31, lambda i: hello(zpeer(flight_order(i)), s))

    def hello_plane(j):
        q = (chip + j) % 16
        for cc in (0, 1):
            fd, sd = on_chip(q, cc)
            hello(fd, sd)

    loop(1, 16, hello_plane)
    hello(f, sib)

    def colblock(xx, yll, cc):
        return (1 - cc) * (4 * yll + xx) + cc * (8 + 2 * xx + yll)

    def wblock(yy, xx, cc):
        cb = colblock(xx, yy % 2, cc)
        return wbuf.at[
            pl.ds(pl.multiple_of((yy // 2) * 160, 32), 160),
            pl.ds(pl.multiple_of(cb * BLK, BLK), BLK),
        ]

    mycol = pl.multiple_of(colblock(x, yl, c) * BLK, BLK)
    wpad[...] = jnp.zeros((8, COLS), F32)
    loads[0].wait()
    loads[1].wait()
    wpad[0:5, 0 : 9 * CH] = ws_ref[...].astype(F32)
    wpad[0:5, TIME_AT : TIME_AT + 3 * CH] = wt_ref[...].astype(F32)
    zbuf[z] = wpad[:, pl.ds(mycol, BLK)].astype(BF16)

    pix = lax.broadcasted_iota(jnp.int32, (1, PIXELS), 1)
    col = pix - WIDTH * ((pix * 2731) >> 16)

    def inside(a, b):
        ok = pix >= 0
        if a == 0:
            ok = ok & (pix >= WIDTH)
        if a == 2:
            ok = ok & (pix < PIXELS - WIDTH)
        if b == 0:
            ok = ok & (col >= 1)
        if b == 2:
            ok = ok & (col <= WIDTH - 2)
        return ok

    def moved(values, a, b):
        step = WIDTH * (a - 1) + b - 1
        if step == 0:
            return values
        return jnp.where(inside(a, b), pltpu.roll(values, (-step) % PIXELS, 1), 0.0)

    loads[2].wait()
    inp = x_ref[...].astype(F32)
    for a in range(3):
        for b in range(3):
            at = (3 * a + b) * CH
            xcol[at : at + CH, :] = moved(inp, a, b).astype(BF16)
    xcol[9 * CH :, :] = jnp.zeros((TIME_AT - 9 * CH, PIXELS), BF16)

    loads[3].wait()
    pl.semaphore_wait(barrier, 62)

    def zw_copy(d, slot):
        return copy(zbuf.at[slot], zbuf.at[slot], zw_s.at[d], zw_r.at[d], zpeer(d), s)

    loop(0, 31, lambda i: zw_copy(flight_order(i), z).start())
    pending.append(lambda: loop(1, 32, lambda d: zw_copy(d, z).wait_send()))
    rim_up = copy(og_ref, ogr.at[0], rim_s.at[0], rim_r.at[0], f, (s + 1) % 16)
    rim_down = copy(og_ref, ogr.at[1], rim_s.at[1], rim_r.at[1], f, (s + 15) % 16)
    start(rim_up)
    start(rim_down)
    loop(1, 32, lambda d: zw_copy(d, (z - d + NZ) % NZ).wait_recv())

    slot = lax.broadcasted_iota(jnp.int32, (160, 256), 1)
    row = lax.broadcasted_iota(jnp.int32, (160, 256), 0)
    pick = jnp.where(((slot >> 3) * 5 + (slot & 7) == row) & ((slot & 7) < 5), 1.0, 0.0).astype(BF16)
    pieces = zbuf[...].astype(F32).reshape(256, BLK).astype(BF16)
    wbuf[pl.ds(pl.multiple_of(yh * 160, 32), 160), pl.ds(mycol, BLK)] = nn(pick, pieces).astype(BF16)

    def to_sibling(ref, n):
        start(copy(ref, ref, p3_s.at[n], p3_r.at[n], f, sib))

    def first_block(i):
        return (y - c * i + 4) % 4, (x - (1 - c) * i + 4) % 4

    def second_block(i, j, cc):
        return (y - (1 - cc) * j - cc * i + 8) % 4, (x - cc * j - (1 - cc) * i + 8) % 4

    mine = wblock(y, x, c)
    for j in range(1, 4):
        fd, sd = on_chip(((y + c * j) % 4) * 4 + (x + (1 - c) * j) % 4, c)
        start(copy(mine, mine, p1_s.at[j], p1_r.at[j], fd, sd))
    for i in range(4):
        by, bx = first_block(i)
        ref = wblock(by, bx, c)
        if i:
            copy(ref, ref, p1_s.at[i], p1_r.at[i], f, sib).wait_recv()
        for j in range(1, 4):
            fd, sd = on_chip(((y + (1 - c) * j) % 4) * 4 + (x + c * j) % 4, c)
            start(copy(ref, ref, p2_s.at[4 * j + i], p2_r.at[4 * j + i], fd, sd))
        to_sibling(ref, i)
    for i in range(4):
        for j in range(1, 4):
            by, bx = second_block(i, j, c)
            ref = wblock(by, bx, c)
            copy(ref, ref, p2_s.at[4 * j + i], p2_r.at[4 * j + i], f, sib).wait_recv()
            to_sibling(ref, 4 * j + i)
    for n in range(16):
        by, bx = second_block(n % 4, n // 4, 1 - c)
        ref = wblock(by, bx, 1 - c)
        copy(ref, ref, p3_s.at[n], p3_r.at[n], f, sib).wait_recv()

    def lane_sums(values):
        part = values[:, 0:128] + values[:, 128:256] + values[:, 256:384]
        return jnp.sum(part.T, axis=0, keepdims=True)

    def sums_of(first, second):
        return jnp.concatenate([lane_sums(first), lane_sums(second)], axis=0)

    def exchange(buf, value, send, recv):
        buf[s] = value

        def go(j):
            return copy(buf.at[s], buf.at[s], send.at[j], recv.at[j], f, (s + j) % 16)

        loop(1, 16, lambda j: go(j).start())
        pending.append(lambda: loop(1, 16, lambda j: go(j).wait_send()))

    def arrived(buf, send, recv):
        def take(j):
            src = (s - j + 16) % 16
            copy(buf.at[src], buf.at[src], send.at[j], recv.at[j], f, src).wait_recv()

        loop(1, 16, take)

    hidden = nn(wbuf[:, 0:TIME_AT], xcol[...])
    exchange(st1, sums_of(hidden, hidden * hidden), st1_s, st1_r)

    has_left = jnp.where(s > 0, 1.0, 0.0)
    has_right = jnp.where(s < FRAMES - 1, 1.0, 0.0)
    rim_up.wait_recv()
    rim_down.wait_recv()
    wtime = wbuf[:, TIME_AT:COLS]
    taps = [wtime[:, k * CH : (k + 1) * CH] for k in range(3)]
    grads = (ogr[1], og_ref[...], ogr[0])
    act_grad = (
        (
            nn(taps[0].T, grads[0]) * has_right
            + nn(taps[1].T, grads[1])
            + nn(taps[2].T, grads[2]) * has_left
        )
        .astype(BF16)
        .astype(F32)
    )
    per = CH // GROUPS
    row_i = lax.broadcasted_iota(jnp.int32, (CH, CH), 0)
    col_i = lax.broadcasted_iota(jnp.int32, (CH, CH), 1)
    low = row_i - (row_i % per)
    same = jnp.where((col_i >= low) & (col_i < low + per), 1.0, 0.0)
    counted = float(FRAMES * PIXELS * per)

    def group_means(buf):
        grouped = lax.dot_general(
            same,
            jnp.sum(buf[...], axis=0),
            (((1,), (1,)), ((), ())),
            precision=lax.Precision.HIGHEST,
            preferred_element_type=F32,
        )
        return grouped[:, 0:1] / counted, grouped[:, 1:2] / counted

    def column(ref):
        return jnp.broadcast_to(ref[...].reshape(1, CH), (8, CH)).T[:, 0:1]

    gain = column(gain_ref)
    shift = column(shift_ref)

    arrived(st1, st1_s, st1_r)
    average, squares = group_means(st1)
    inv_std = lax.rsqrt(squares - average * average + EPSILON)
    normed = (hidden - average) * inv_std
    preact = normed * gain + shift
    sig = 1.0 / (1.0 + jnp.exp(-preact))
    activation = (preact * sig).astype(BF16)
    act_ref[...] = activation

    def share_of(part):
        pieces = []
        for k, weight in enumerate((has_right, None, has_left)):
            ref = (ogr.at[1], og_ref, ogr.at[0])[k]
            rows = jnp.concatenate(
                [ref[pl.ds(pl.multiple_of(160 * h + 80 * part, 16), 80), :] for h in range(2)], axis=0
            )
            piece = nt(rows, activation)
            pieces.append(piece if weight is None else piece * weight)
        pieces.append(jnp.zeros((160, 64), F32))
        return jnp.concatenate(pieces, axis=1).reshape(2, 80, 1024)

    gout[...] = share_of(1 - c).astype(BF16)
    core_copy = copy(gout, gsib, gc_s.at[0], gc_r.at[0], f, sib)
    start(core_copy)
    own_share = share_of(c)

    core_copy.wait_recv()
    gchip[...] = (own_share + gsib[...].astype(F32)).astype(BF16)

    def tile_of(q):
        return gchip.at[q // 8, :, pl.ds(pl.multiple_of((q % 8) * 128, 128), 128)]

    def gp_copy(j, to, src):
        fd, sd = on_chip(to, c)
        return copy(tile_of(to), gplane.at[src], gp_s.at[j], gp_r.at[j], fd, sd)

    loop(1, 16, lambda j: gp_copy(j, (chip + j) % 16, chip).start())
    pending.append(lambda: loop(1, 16, lambda j: gp_copy(j, (chip + j) % 16, chip).wait_send()))
    gplane[chip] = gchip[chip // 8, :, pl.ds(pl.multiple_of((chip % 8) * 128, 128), 128)]

    scaled = act_grad * (sig * (1.0 + preact * (1.0 - sig))) * gain
    exchange(st2, sums_of(scaled, scaled * normed), st2_s, st2_r)
    arim_up = copy(act_ref, actr.at[0], arim_s.at[0], arim_r.at[0], f, (s + 1) % 16)
    arim_down = copy(act_ref, actr.at[1], arim_s.at[1], arim_r.at[1], f, (s + 15) % 16)
    start(arim_up)
    start(arim_down)

    arrived(st2, st2_s, st2_r)
    mean_one, mean_two = group_means(st2)
    hid_grad = (inv_std * (scaled - mean_one - normed * mean_two)).astype(BF16)

    def gp_take(j):
        src = (chip - j + 16) % 16
        gp_copy(j, src, src).wait_recv()

    loop(1, 16, gp_take)
    share = jnp.zeros((80, 128), F32)
    for i in range(16):
        share = share + gplane[i].astype(F32)

    slot = lax.broadcasted_iota(jnp.int32, (128, 80), 0)
    row = lax.broadcasted_iota(jnp.int32, (128, 80), 1)
    put = jnp.where(((slot >> 3) * 5 + (slot & 7) == row) & ((slot & 7) < 5), 1.0, 0.0).astype(BF16)
    zsend[...] = nn(put, share.astype(BF16)).reshape(16, 8, 128).astype(BF16)
    owner = z // 16 == c

    def gz_copy(d):
        return copy(zsend.at[(z + d) % 16], zrecv.at[d], gz_s.at[d], gz_r.at[d], zpeer(d), s)

    def to_owner(d, act):
        @pl.when(((z + d) % NZ) // 16 == c)
        def _():
            act(gz_copy(d))

    loop(0, 31, lambda i: to_owner(flight_order(i), lambda cp: cp.start()))
    pending.append(lambda: loop(1, 32, lambda d: to_owner(d, lambda cp: cp.wait_send())))

    wtrans[...] = wbuf[:, 0:TIME_AT].T
    total = nn(wtrans[4 * CH : 5 * CH, :], hid_grad)
    for a in range(3):
        for b in range(3):
            if a != 1 or b != 1:
                at = (3 * a + b) * CH
                total = total + moved(nn(wtrans[at : at + CH, :], hid_grad), 2 - a, 2 - b)
    ing_ref[...] = total.astype(BF16)
    ing_out = pltpu.make_async_copy(ing_ref, ing_hbm, out_sem.at[0])
    ing_out.start()
    arim_up.wait_recv()
    arim_down.wait_recv()
    mixed_ref[...] = (
        nn(taps[0], actr[0]) * has_left + nn(taps[1], act_ref[...]) + nn(taps[2], actr[1]) * has_right
    ).astype(BF16)

    mixed_out = pltpu.make_async_copy(mixed_ref, mixed_hbm, out_sem.at[1])
    mixed_out.start()

    def fin_copy(j, src):
        return copy(fval, fin.at[src], fin_s.at[j], fin_r.at[src], f, (s + j) % 16)

    @pl.when(owner)
    def _():
        zrecv[0] = zsend[z % 16]
        loop(1, 32, lambda d: gz_copy(d).wait_recv())
        last = jnp.sum(zrecv[...].astype(F32), axis=0) * (1.0 / (lax.axis_size("fsdp") * FRAMES))
        fval[...] = last
        loop(1, 16, lambda j: fin_copy(j, chip % 8).start())
        fin[chip % 8] = last

    def fin_take(src):
        @pl.when(jnp.logical_not(owner) | (src != chip % 8))
        def _():
            fin_copy(1, src).wait_recv()

    loop(0, 8, fin_take)
    gt_ref[...] = jnp.concatenate([fin[t] for t in range(8)], axis=1)[0:5, 0 : 3 * CH]
    gt_out = pltpu.make_async_copy(gt_ref, gt_hbm, out_sem.at[2])
    gt_out.start()

    @pl.when(owner)
    def _():
        loop(1, 16, lambda j: fin_copy(j, chip % 8).wait_send())

    for left_over in pending:
        left_over()
    ing_out.wait()
    mixed_out.wait()
    gt_out.wait()


def hand_over(mixed_in, ing_in, gt_in, mixed_out, ing_out, gt_out, sems):
    copies = [
        pltpu.make_async_copy(src, dst, sems.at[n])
        for n, (src, dst) in enumerate(((mixed_in, mixed_out), (ing_in, ing_out), (gt_in, gt_out)))
    ]
    for cp in copies:
        cp.start()
    for cp in copies:
        cp.wait()


def local(clips_in, weight_space, weight_time, norm_gain, norm_shift, out_grad):
    vmem = pl.BlockSpec(memory_space=pltpu.VMEM)
    dma = pltpu.SemaphoreType.DMA
    hbm = pl.BlockSpec(memory_space=pl.ANY)
    results = pl.pallas_call(
        kernel,
        out_shape=(
            jax.ShapeDtypeStruct((CH, PIXELS), BF16),
            jax.ShapeDtypeStruct((CH, PIXELS), BF16),
            jax.ShapeDtypeStruct((5, 3 * CH), F32),
        ),
        in_specs=[hbm, hbm, hbm, vmem, vmem, hbm],
        out_specs=(hbm, hbm, hbm),
        scratch_shapes=[
            pltpu.VMEM((CH, PIXELS), BF16),
            pltpu.VMEM((5, 9 * CH), BF16),
            pltpu.VMEM((5, 3 * CH), BF16),
            pltpu.VMEM((CH, PIXELS), BF16),
            pltpu.VMEM((CH, PIXELS), BF16),
            pltpu.VMEM((CH, PIXELS), BF16),
            pltpu.VMEM((5, 3 * CH), F32),
            pltpu.VMEM((2, CH, PIXELS), BF16),
            pltpu.VMEM((8, COLS), F32),
            pltpu.VMEM((NZ, 8, BLK), BF16),
            pltpu.VMEM((CH, COLS), BF16),
            pltpu.VMEM((TIME_AT, PIXELS), BF16),
            pltpu.VMEM((16, 2, CH), F32),
            pltpu.VMEM((16, 2, CH), F32),
            pltpu.VMEM((CH, PIXELS), BF16),
            pltpu.VMEM((2, CH, PIXELS), BF16),
            pltpu.VMEM((2, 80, 1024), BF16),
            pltpu.VMEM((2, 80, 1024), BF16),
            pltpu.VMEM((2, 80, 1024), BF16),
            pltpu.VMEM((16, 80, 128), BF16),
            pltpu.VMEM((16, 8, 128), BF16),
            pltpu.VMEM((NZ, 8, 128), BF16),
            pltpu.VMEM((8, 128), F32),
            pltpu.VMEM((8, 8, 128), F32),
            pltpu.VMEM((TIME_AT, CH), BF16),
        ]
        + [dma((n,)) for n in (2, 2, NZ, NZ, 4, 4)]
        + [dma((16,))] * 8
        + [dma((2,))] * 2
        + [dma((1,))] * 2
        + [dma((16,))] * 2
        + [dma((NZ,))] * 2
        + [dma((16,)), dma((8,)), dma((4,)), dma((3,))],
        compiler_params=pltpu.CompilerParams(
            collective_id=0, has_side_effects=True, vmem_limit_bytes=56 * 1024 * 1024
        ),
    )(
        clips_in.reshape(PIXELS, CH).T,
        weight_space,
        weight_time,
        norm_gain,
        norm_shift,
        out_grad.reshape(PIXELS, CH).T,
    )
    mixed, in_grad, grad_time = pl.pallas_call(
        hand_over,
        out_shape=tuple(jax.ShapeDtypeStruct(v.shape, v.dtype) for v in results),
        in_specs=[hbm] * 3,
        out_specs=(hbm,) * 3,
        scratch_shapes=[dma((3,))],
    )(*results)
    return mixed.T.reshape(clips_in.shape), in_grad.T.reshape(clips_in.shape), grad_time


def solution(mesh):
    in_specs = (
        P("fsdp", "seq", None, None),
        P("fsdp", None),
        P("fsdp", None),
        P(),
        P(),
        P("fsdp", "seq", None, None),
    )
    out_specs = (P("fsdp", "seq", None, None), P("fsdp", "seq", None, None), P("fsdp", None))
    return jax.shard_map(local, mesh=mesh, in_specs=in_specs, out_specs=out_specs, check_vma=False)
```

```python
import jax
import jax.numpy as jnp
from jax import lax
from jax.experimental import pallas as pl
from jax.experimental.pallas import tpu as pltpu
from jax.sharding import PartitionSpec as P

GROUPS = 32
FRAMES = 16
HEIGHT = 16
WIDTH = 24
PIXELS = HEIGHT * WIDTH
CH = 320
EPSILON = 1e-05
NZ = 32
TIME_AT = 3072
COLS = 4096
BLK = 256
MESH = pl.DeviceIdType.MESH
F32 = jnp.float32
BF16 = jnp.bfloat16


def nt(left, right):
    return lax.dot_general(left, right, (((1,), (1,)), ((), ())), preferred_element_type=F32)


def nn(left, right):
    return lax.dot_general(left, right, (((1,), (0,)), ((), ())), preferred_element_type=F32)


def flight_order(i):
    half = (i + 1) // 2
    return 16 + half * (1 - 2 * (i % 2))


def kernel(
    x_hbm,
    ws_hbm,
    wt_hbm,
    gain_hbm,
    shift_hbm,
    og_hbm,
    mixed_hbm,
    ing_hbm,
    gt_hbm,
    x_ref,
    ws_ref,
    wt_ref,
    gain_ref,
    shift_ref,
    og_ref,
    mixed_ref,
    ing_ref,
    gt_ref,
    ogr,
    wpad,
    zbuf,
    wbuf,
    xcol,
    st1,
    st2,
    act_ref,
    actr,
    gout,
    gsib,
    gchip,
    gplane,
    zsend,
    zrecv,
    fval,
    fin,
    wtrans,
    rim_s,
    rim_r,
    zw_s,
    zw_r,
    p1_s,
    p1_r,
    p2_s,
    p2_r,
    p3_s,
    p3_r,
    st1_s,
    st1_r,
    st2_s,
    st2_r,
    arim_s,
    arim_r,
    gc_s,
    gc_r,
    gp_s,
    gp_r,
    gz_s,
    gz_r,
    fin_s,
    fin_r,
    in_sem,
    out_sem,
):
    f = lax.axis_index("fsdp")
    s = lax.axis_index("seq")
    z = f % NZ
    yh = f // NZ
    c = s % 2
    x = (s // 2) % 4
    yl = s // 8
    y = yh * 2 + yl
    chip = y * 4 + x
    sib = s + 1 - 2 * c
    pending = []

    loads = [
        pltpu.make_async_copy(src, dst, in_sem.at[n])
        for n, (src, dst) in enumerate(
            (
                (ws_hbm, ws_ref),
                (wt_hbm, wt_ref),
                (x_hbm, x_ref),
                (og_hbm, og_ref),
                (gain_hbm, gain_ref),
                (shift_hbm, shift_ref),
            )
        )
    ]
    for load in loads:
        load.start()

    def copy(src, dst, send, recv, fdev, sdev):
        return pltpu.make_async_remote_copy(
            src_ref=src,
            dst_ref=dst,
            send_sem=send,
            recv_sem=recv,
            device_id=(fdev, sdev),
            device_id_type=MESH,
        )

    def start(cp):
        cp.start()
        pending.append(cp.wait_send)

    def loop(low, high, body):
        def step(i, carry):
            body(i)
            return carry

        lax.fori_loop(low, high, step, 0)

    def zpeer(d):
        return yh * NZ + (z + d) % NZ

    def on_chip(q, cc):
        return (q // 8) * NZ + z, ((q // 4) % 2) * 8 + (q % 4) * 2 + cc

    barrier = pltpu.get_barrier_semaphore()

    def hello(fdev, sdev):
        pl.semaphore_signal(barrier, inc=1, device_id=(fdev, sdev), device_id_type=MESH)

    loop(0, 31, lambda i: hello(zpeer(flight_order(i)), s))

    def hello_plane(j):
        q = (chip + j) % 16
        for cc in (0, 1):
            fd, sd = on_chip(q, cc)
            hello(fd, sd)

    loop(1, 16, hello_plane)
    hello(f, sib)

    def colblock(xx, yll, cc):
        last = xx // 3
        return (1 - last) * (6 * cc + 3 * yll + xx) + last * (12 + 2 * cc + yll)

    def wblock(yy, xx, cc):
        cb = colblock(xx, yy % 2, cc)
        return wbuf.at[
            pl.ds(pl.multiple_of((yy // 2) * 160, 32), 160),
            pl.ds(pl.multiple_of(cb * BLK, BLK), BLK),
        ]

    mycol = pl.multiple_of(colblock(x, yl, c) * BLK, BLK)
    wpad[...] = jnp.zeros((8, COLS), F32)
    loads[0].wait()
    loads[1].wait()
    wpad[0:5, 0 : 9 * CH] = ws_ref[...].astype(F32)
    wpad[0:5, TIME_AT : TIME_AT + 3 * CH] = wt_ref[...].astype(F32)
    zbuf[z] = wpad[:, pl.ds(mycol, BLK)].astype(BF16)

    pix = lax.broadcasted_iota(jnp.int32, (1, PIXELS), 1)
    col = pix - WIDTH * ((pix * 2731) >> 16)

    def inside(a, b):
        ok = pix >= 0
        if a == 0:
            ok = ok & (pix >= WIDTH)
        if a == 2:
            ok = ok & (pix < PIXELS - WIDTH)
        if b == 0:
            ok = ok & (col >= 1)
        if b == 2:
            ok = ok & (col <= WIDTH - 2)
        return ok

    def moved(values, a, b):
        step = WIDTH * (a - 1) + b - 1
        if step == 0:
            return values
        return jnp.where(inside(a, b), pltpu.roll(values, (-step) % PIXELS, 1), 0.0)

    loads[2].wait()
    inp = x_ref[...].astype(F32)
    for a in range(3):
        for b in range(3):
            at = (3 * a + b) * CH
            xcol[at : at + CH, :] = moved(inp, a, b).astype(BF16)
    xcol[9 * CH :, :] = jnp.zeros((TIME_AT - 9 * CH, PIXELS), BF16)

    for load in loads[3:]:
        load.wait()
    pl.semaphore_wait(barrier, 62)

    def zw_copy(d, slot):
        return copy(zbuf.at[slot], zbuf.at[slot], zw_s.at[d], zw_r.at[d], zpeer(d), s)

    loop(0, 31, lambda i: zw_copy(flight_order(i), z).start())
    pending.append(lambda: loop(1, 32, lambda d: zw_copy(d, z).wait_send()))
    rim_up = copy(og_ref, ogr.at[0], rim_s.at[0], rim_r.at[0], f, (s + 1) % 16)
    rim_down = copy(og_ref, ogr.at[1], rim_s.at[1], rim_r.at[1], f, (s + 15) % 16)
    start(rim_up)
    start(rim_down)
    loop(1, 32, lambda d: zw_copy(d, (z - d + NZ) % NZ).wait_recv())

    slot = lax.broadcasted_iota(jnp.int32, (160, 256), 1)
    row = lax.broadcasted_iota(jnp.int32, (160, 256), 0)
    pick = jnp.where(((slot >> 3) * 5 + (slot & 7) == row) & ((slot & 7) < 5), 1.0, 0.0).astype(BF16)
    pieces = zbuf[...].astype(F32).reshape(256, BLK).astype(BF16)
    wbuf[pl.ds(pl.multiple_of(yh * 160, 32), 160), pl.ds(mycol, BLK)] = nn(pick, pieces).astype(BF16)

    def to_sibling(i, j):
        ref = wblock(*second_block(i, j, c), c)
        n = 4 * j + i
        return copy(ref, ref, p3_s.at[n], p3_r.at[n], f, sib)

    def onward(i, j):
        ref = wblock(*first_block(i), c)
        n = 4 * j + i
        fd, sd = on_chip(((y + (1 - c) * j) % 4) * 4 + (x + c * j) % 4, c)
        return copy(ref, ref, p2_s.at[n], p2_r.at[n], fd, sd)

    def first_block(i):
        return (y - c * i + 4) % 4, (x - (1 - c) * i + 4) % 4

    def second_block(i, j, cc):
        return (y - (1 - cc) * j - cc * i + 8) % 4, (x - cc * j - (1 - cc) * i + 8) % 4

    mine = wblock(y, x, c)
    for j in range(1, 4):
        fd, sd = on_chip(((y + c * j) % 4) * 4 + (x + (1 - c) * j) % 4, c)
        start(copy(mine, mine, p1_s.at[j], p1_r.at[j], fd, sd))
    def forward(i):
        for j in range(1, 4):
            onward(i, j).start()
        to_sibling(i, 0).start()

    for i in range(4):
        if i:
            ref = wblock(*first_block(i), c)
            copy(ref, ref, p1_s.at[i], p1_r.at[i], f, sib).wait_recv()
        pl.when(first_block(i)[1] < 3)(lambda i=i: forward(i))
    for i in range(4):
        pl.when(first_block(i)[1] == 3)(lambda i=i: forward(i))

    def second(i, j):
        ref = wblock(*second_block(i, j, c), c)
        n = 4 * j + i
        copy(ref, ref, p2_s.at[n], p2_r.at[n], f, sib).wait_recv()
        to_sibling(i, j).start()

    def from_sibling(i, j):
        ref = wblock(*second_block(i, j, 1 - c), 1 - c)
        n = 4 * j + i
        copy(ref, ref, p3_s.at[n], p3_r.at[n], f, sib).wait_recv()

    def take_blocks(temporal):
        def wanted(bx):
            return bx == 3 if temporal else bx < 3

        for i in range(4):
            for j in range(1, 4):
                pl.when(wanted(second_block(i, j, c)[1]))(lambda i=i, j=j: second(i, j))
        for i in range(4):
            for j in range(4):
                pl.when(wanted(second_block(i, j, 1 - c)[1]))(lambda i=i, j=j: from_sibling(i, j))

    def blocks_gone():
        for i in range(4):
            for j in range(4):
                if j:
                    onward(i, j).wait_send()
                to_sibling(i, j).wait_send()

    pending.append(blocks_gone)
    take_blocks(False)

    def lane_sums(values):
        part = values[:, 0:128] + values[:, 128:256] + values[:, 256:384]
        return jnp.sum(part.T, axis=0, keepdims=True)

    def sums_of(first, second):
        return jnp.concatenate([lane_sums(first), lane_sums(second)], axis=0)

    def exchange(buf, value, send, recv):
        buf[s] = value

        def go(j):
            return copy(buf.at[s], buf.at[s], send.at[j], recv.at[j], f, (s + j) % 16)

        loop(1, 16, lambda j: go(j).start())
        pending.append(lambda: loop(1, 16, lambda j: go(j).wait_send()))

    def arrived(buf, send, recv):
        def take(j):
            src = (s - j + 16) % 16
            copy(buf.at[src], buf.at[src], send.at[j], recv.at[j], f, src).wait_recv()

        loop(1, 16, take)

    hidden = nn(wbuf[:, 0:TIME_AT], xcol[...])
    exchange(st1, sums_of(hidden, hidden * hidden), st1_s, st1_r)

    has_left = jnp.where(s > 0, 1.0, 0.0)
    has_right = jnp.where(s < FRAMES - 1, 1.0, 0.0)
    rim_up.wait_recv()
    rim_down.wait_recv()
    take_blocks(True)
    wtime = wbuf[:, TIME_AT:COLS]
    taps = [wtime[:, k * CH : (k + 1) * CH] for k in range(3)]
    grads = (ogr[1], og_ref[...], ogr[0])
    act_grad = (
        (
            nn(taps[0].T, grads[0]) * has_right
            + nn(taps[1].T, grads[1])
            + nn(taps[2].T, grads[2]) * has_left
        )
        .astype(BF16)
        .astype(F32)
    )
    per = CH // GROUPS
    row_i = lax.broadcasted_iota(jnp.int32, (CH, CH), 0)
    col_i = lax.broadcasted_iota(jnp.int32, (CH, CH), 1)
    low = row_i - (row_i % per)
    same = jnp.where((col_i >= low) & (col_i < low + per), 1.0, 0.0)
    counted = float(FRAMES * PIXELS * per)

    def group_means(buf):
        grouped = lax.dot_general(
            same,
            jnp.sum(buf[...], axis=0),
            (((1,), (1,)), ((), ())),
            precision=lax.Precision.HIGHEST,
            preferred_element_type=F32,
        )
        return grouped[:, 0:1] / counted, grouped[:, 1:2] / counted

    def column(ref):
        return jnp.broadcast_to(ref[...].reshape(1, CH), (8, CH)).T[:, 0:1]

    gain = column(gain_ref)
    shift = column(shift_ref)

    arrived(st1, st1_s, st1_r)
    average, squares = group_means(st1)
    inv_std = lax.rsqrt(squares - average * average + EPSILON)
    normed = (hidden - average) * inv_std
    preact = normed * gain + shift
    sig = 1.0 / (1.0 + jnp.exp(-preact))
    activation = (preact * sig).astype(BF16)
    act_ref[...] = activation

    def share_of(part):
        pieces = []
        for k, weight in enumerate((has_right, None, has_left)):
            ref = (ogr.at[1], og_ref, ogr.at[0])[k]
            rows = jnp.concatenate(
                [ref[pl.ds(pl.multiple_of(160 * h + 80 * part, 16), 80), :] for h in range(2)], axis=0
            )
            piece = nt(rows, activation)
            pieces.append(piece if weight is None else piece * weight)
        pieces.append(jnp.zeros((160, 64), F32))
        return jnp.concatenate(pieces, axis=1).reshape(2, 80, 1024)

    gout[...] = share_of(1 - c).astype(BF16)
    core_copy = copy(gout, gsib, gc_s.at[0], gc_r.at[0], f, sib)
    start(core_copy)
    own_share = share_of(c)

    core_copy.wait_recv()
    gchip[...] = (own_share + gsib[...].astype(F32)).astype(BF16)

    def tile_of(q):
        return gchip.at[q // 8, :, pl.ds(pl.multiple_of((q % 8) * 128, 128), 128)]

    def gp_copy(j, to, src):
        fd, sd = on_chip(to, c)
        return copy(tile_of(to), gplane.at[src], gp_s.at[j], gp_r.at[j], fd, sd)

    loop(1, 16, lambda j: gp_copy(j, (chip + j) % 16, chip).start())
    pending.append(lambda: loop(1, 16, lambda j: gp_copy(j, (chip + j) % 16, chip).wait_send()))
    gplane[chip] = gchip[chip // 8, :, pl.ds(pl.multiple_of((chip % 8) * 128, 128), 128)]

    scaled = act_grad * (sig * (1.0 + preact * (1.0 - sig))) * gain
    exchange(st2, sums_of(scaled, scaled * normed), st2_s, st2_r)

    def gp_take(j):
        src = (chip - j + 16) % 16
        gp_copy(j, src, src).wait_recv()

    loop(1, 16, gp_take)
    share = jnp.zeros((80, 128), F32)
    for i in range(16):
        share = share + gplane[i].astype(F32)

    slot = lax.broadcasted_iota(jnp.int32, (128, 80), 0)
    row = lax.broadcasted_iota(jnp.int32, (128, 80), 1)
    put = jnp.where(((slot >> 3) * 5 + (slot & 7) == row) & ((slot & 7) < 5), 1.0, 0.0).astype(BF16)
    zsend[...] = nn(put, share.astype(BF16)).reshape(16, 8, 128).astype(BF16)
    owner = z // 16 == c

    def gz_copy(d):
        return copy(zsend.at[(z + d) % 16], zrecv.at[d], gz_s.at[d], gz_r.at[d], zpeer(d), s)

    def to_owner(d, act):
        @pl.when(((z + d) % NZ) // 16 == c)
        def _():
            act(gz_copy(d))

    loop(0, 31, lambda i: to_owner(flight_order(i), lambda cp: cp.start()))
    pending.append(lambda: loop(1, 32, lambda d: to_owner(d, lambda cp: cp.wait_send())))

    arim_up = copy(act_ref, actr.at[0], arim_s.at[0], arim_r.at[0], f, (s + 1) % 16)
    arim_down = copy(act_ref, actr.at[1], arim_s.at[1], arim_r.at[1], f, (s + 15) % 16)
    start(arim_up)
    start(arim_down)

    arrived(st2, st2_s, st2_r)
    mean_one, mean_two = group_means(st2)
    hid_grad = (inv_std * (scaled - mean_one - normed * mean_two)).astype(BF16)

    wtrans[...] = wbuf[:, 0:TIME_AT].T
    total = nn(wtrans[4 * CH : 5 * CH, :], hid_grad)
    for a in range(3):
        for b in range(3):
            if a != 1 or b != 1:
                at = (3 * a + b) * CH
                total = total + moved(nn(wtrans[at : at + CH, :], hid_grad), 2 - a, 2 - b)
    ing_ref[...] = total.astype(BF16)
    ing_out = pltpu.make_async_copy(ing_ref, ing_hbm, out_sem.at[0])
    ing_out.start()
    arim_up.wait_recv()
    arim_down.wait_recv()
    mixed_ref[...] = (
        nn(taps[0], actr[0]) * has_left + nn(taps[1], act_ref[...]) + nn(taps[2], actr[1]) * has_right
    ).astype(BF16)

    mixed_out = pltpu.make_async_copy(mixed_ref, mixed_hbm, out_sem.at[1])
    mixed_out.start()

    for left_over in pending:
        left_over()

    def fin_copy(j, src):
        return copy(fval, fin.at[src], fin_s.at[j], fin_r.at[src], f, (s + j) % 16)

    @pl.when(owner)
    def _():
        zrecv[0] = zsend[z % 16]
        loop(1, 32, lambda d: gz_copy(d).wait_recv())
        last = jnp.sum(zrecv[...].astype(F32), axis=0) * (1.0 / (lax.axis_size("fsdp") * FRAMES))
        fval[...] = last
        loop(1, 16, lambda j: fin_copy(j, chip % 8).start())
        fin[chip % 8] = last

    def fin_take(src):
        @pl.when(jnp.logical_not(owner) | (src != chip % 8))
        def _():
            fin_copy(1, src).wait_recv()

    loop(0, 8, fin_take)
    gt_ref[...] = jnp.concatenate([fin[t] for t in range(8)], axis=1)[0:5, 0 : 3 * CH]
    gt_out = pltpu.make_async_copy(gt_ref, gt_hbm, out_sem.at[2])
    gt_out.start()

    @pl.when(owner)
    def _():
        loop(1, 16, lambda j: fin_copy(j, chip % 8).wait_send())

    ing_out.wait()
    mixed_out.wait()
    gt_out.wait()


def local(clips_in, weight_space, weight_time, norm_gain, norm_shift, out_grad):
    dma = pltpu.SemaphoreType.DMA
    hbm = pl.BlockSpec(memory_space=pltpu.HBM)
    anywhere = pl.BlockSpec(memory_space=pl.ANY)
    mixed, in_grad, grad_time = pl.pallas_call(
        kernel,
        out_shape=(
            jax.ShapeDtypeStruct((CH, PIXELS), BF16),
            jax.ShapeDtypeStruct((CH, PIXELS), BF16),
            jax.ShapeDtypeStruct((5, 3 * CH), F32),
        ),
        in_specs=[hbm] * 6,
        out_specs=(anywhere, anywhere, anywhere),
        scratch_shapes=[
            pltpu.VMEM((CH, PIXELS), BF16),
            pltpu.VMEM((5, 9 * CH), BF16),
            pltpu.VMEM((5, 3 * CH), BF16),
            pltpu.VMEM((CH,), F32),
            pltpu.VMEM((CH,), F32),
            pltpu.VMEM((CH, PIXELS), BF16),
            pltpu.VMEM((CH, PIXELS), BF16),
            pltpu.VMEM((CH, PIXELS), BF16),
            pltpu.VMEM((5, 3 * CH), F32),
            pltpu.VMEM((2, CH, PIXELS), BF16),
            pltpu.VMEM((8, COLS), F32),
            pltpu.VMEM((NZ, 8, BLK), BF16),
            pltpu.VMEM((CH, COLS), BF16),
            pltpu.VMEM((TIME_AT, PIXELS), BF16),
            pltpu.VMEM((16, 2, CH), F32),
            pltpu.VMEM((16, 2, CH), F32),
            pltpu.VMEM((CH, PIXELS), BF16),
            pltpu.VMEM((2, CH, PIXELS), BF16),
            pltpu.VMEM((2, 80, 1024), BF16),
            pltpu.VMEM((2, 80, 1024), BF16),
            pltpu.VMEM((2, 80, 1024), BF16),
            pltpu.VMEM((16, 80, 128), BF16),
            pltpu.VMEM((16, 8, 128), BF16),
            pltpu.VMEM((NZ, 8, 128), BF16),
            pltpu.VMEM((8, 128), F32),
            pltpu.VMEM((8, 8, 128), F32),
            pltpu.VMEM((TIME_AT, CH), BF16),
        ]
        + [dma((n,)) for n in (2, 2, NZ, NZ, 4, 4)]
        + [dma((16,))] * 8
        + [dma((2,))] * 2
        + [dma((1,))] * 2
        + [dma((16,))] * 2
        + [dma((NZ,))] * 2
        + [dma((16,)), dma((8,)), dma((6,)), dma((3,))],
        compiler_params=pltpu.CompilerParams(
            collective_id=0, has_side_effects=True, vmem_limit_bytes=24 * 1024 * 1024
        ),
    )(
        *(
            pltpu.with_memory_space_constraint(v, pltpu.HBM)
            for v in (
                clips_in.reshape(PIXELS, CH).T,
                weight_space,
                weight_time,
                norm_gain,
                norm_shift,
                out_grad.reshape(PIXELS, CH).T,
            )
        )
    )
    return mixed.T.reshape(clips_in.shape), in_grad.T.reshape(clips_in.shape), grad_time


def solution(mesh):
    in_specs = (
        P("fsdp", "seq", None, None),
        P("fsdp", None),
        P("fsdp", None),
        P(),
        P(),
        P("fsdp", "seq", None, None),
    )
    out_specs = (P("fsdp", "seq", None, None), P("fsdp", "seq", None, None), P("fsdp", None))
    return jax.shard_map(local, mesh=mesh, in_specs=in_specs, out_specs=out_specs, check_vma=False)
```

```python
import jax
import jax.numpy as jnp
from jax import lax
from jax.experimental import pallas as pl
from jax.experimental.pallas import tpu as pltpu
from jax.sharding import PartitionSpec as P

GROUPS = 32
FRAMES = 16
HEIGHT = 16
WIDTH = 24
PIXELS = HEIGHT * WIDTH
CH = 320
EPSILON = 1e-05
NZ = 32
TIME_AT = 3072
COLS = 4096
BLK = 256
MESH = pl.DeviceIdType.MESH
F32 = jnp.float32
BF16 = jnp.bfloat16


def nt(left, right):
    return lax.dot_general(left, right, (((1,), (1,)), ((), ())), preferred_element_type=F32)


def nn(left, right):
    return lax.dot_general(left, right, (((1,), (0,)), ((), ())), preferred_element_type=F32)


def flight_order(i):
    half = (i + 1) // 2
    return 16 + half * (1 - 2 * (i % 2))


def kernel(
    x_hbm,
    ws_hbm,
    wt_hbm,
    gain_hbm,
    shift_hbm,
    og_hbm,
    mixed_hbm,
    ing_hbm,
    gt_hbm,
    x_ref,
    ws_ref,
    wt_ref,
    gain_ref,
    shift_ref,
    og_ref,
    mixed_ref,
    ing_ref,
    gt_ref,
    ogr,
    wpad,
    zbuf,
    wbuf,
    xcol,
    st1,
    st2,
    act_ref,
    actr,
    gout,
    gsib,
    gchip,
    gplane,
    zsend,
    zrecv,
    fval,
    fin,
    wtrans,
    rim_s,
    rim_r,
    zw_s,
    zw_r,
    p1_s,
    p1_r,
    p2_s,
    p2_r,
    p3_s,
    p3_r,
    st1_s,
    st1_r,
    st2_s,
    st2_r,
    arim_s,
    arim_r,
    gc_s,
    gc_r,
    gp_s,
    gp_r,
    gz_s,
    gz_r,
    fin_s,
    fin_r,
    in_sem,
    out_sem,
):
    f = lax.axis_index("fsdp")
    s = lax.axis_index("seq")
    z = f % NZ
    yh = f // NZ
    c = s % 2
    x = (s // 2) % 4
    yl = s // 8
    y = yh * 2 + yl
    chip = y * 4 + x
    sib = s + 1 - 2 * c
    pending = []

    loads = [
        pltpu.make_async_copy(src, dst, in_sem.at[n])
        for n, (src, dst) in enumerate(
            (
                (ws_hbm, ws_ref),
                (wt_hbm, wt_ref),
                (x_hbm, x_ref),
                (og_hbm, og_ref),
                (gain_hbm, gain_ref),
                (shift_hbm, shift_ref),
            )
        )
    ]
    for load in loads:
        load.start()

    def copy(src, dst, send, recv, fdev, sdev):
        return pltpu.make_async_remote_copy(
            src_ref=src,
            dst_ref=dst,
            send_sem=send,
            recv_sem=recv,
            device_id=(fdev, sdev),
            device_id_type=MESH,
        )

    def start(cp):
        cp.start()
        pending.append(cp.wait_send)

    def loop(low, high, body):
        def step(i, carry):
            body(i)
            return carry

        lax.fori_loop(low, high, step, 0)

    def zpeer(d):
        return yh * NZ + (z + d) % NZ

    def on_chip(q, cc):
        return (q // 8) * NZ + z, ((q // 4) % 2) * 8 + (q % 4) * 2 + cc

    barrier = pltpu.get_barrier_semaphore()

    def hello(fdev, sdev):
        pl.semaphore_signal(barrier, inc=1, device_id=(fdev, sdev), device_id_type=MESH)

    loop(0, 31, lambda i: hello(zpeer(flight_order(i)), s))

    def hello_plane(j):
        q = (chip + j) % 16
        for cc in (0, 1):
            fd, sd = on_chip(q, cc)
            hello(fd, sd)

    loop(1, 16, hello_plane)
    hello(f, sib)

    def colblock(xx, yll, cc):
        last = xx // 3
        return (1 - last) * (6 * cc + 3 * yll + xx) + last * (12 + 2 * cc + yll)

    def wblock(yy, xx, cc):
        cb = colblock(xx, yy % 2, cc)
        return wbuf.at[
            pl.ds(pl.multiple_of((yy // 2) * 160, 32), 160),
            pl.ds(pl.multiple_of(cb * BLK, BLK), BLK),
        ]

    mycol = pl.multiple_of(colblock(x, yl, c) * BLK, BLK)
    wpad[...] = jnp.zeros((8, COLS), F32)
    loads[0].wait()
    loads[1].wait()
    wpad[0:5, 0 : 9 * CH] = ws_ref[...].astype(F32)
    wpad[0:5, TIME_AT : TIME_AT + 3 * CH] = wt_ref[...].astype(F32)
    zbuf[z] = wpad[:, pl.ds(mycol, BLK)].astype(BF16)

    pix = lax.broadcasted_iota(jnp.int32, (1, PIXELS), 1)
    col = pix - WIDTH * ((pix * 2731) >> 16)

    def inside(a, b):
        ok = pix >= 0
        if a == 0:
            ok = ok & (pix >= WIDTH)
        if a == 2:
            ok = ok & (pix < PIXELS - WIDTH)
        if b == 0:
            ok = ok & (col >= 1)
        if b == 2:
            ok = ok & (col <= WIDTH - 2)
        return ok

    def moved(values, a, b):
        step = WIDTH * (a - 1) + b - 1
        if step == 0:
            return values
        return jnp.where(inside(a, b), pltpu.roll(values, (-step) % PIXELS, 1), 0.0)

    loads[2].wait()
    inp = x_ref[...].astype(F32)
    for a in range(3):
        for b in range(3):
            at = (3 * a + b) * CH
            xcol[at : at + CH, :] = moved(inp, a, b).astype(BF16)
    xcol[9 * CH :, :] = jnp.zeros((TIME_AT - 9 * CH, PIXELS), BF16)

    for load in loads[3:]:
        load.wait()
    pl.semaphore_wait(barrier, 62)

    def zw_copy(d, slot):
        return copy(zbuf.at[slot], zbuf.at[slot], zw_s.at[d], zw_r.at[d], zpeer(d), s)

    loop(0, 31, lambda i: zw_copy(flight_order(i), z).start())
    pending.append(lambda: loop(1, 32, lambda d: zw_copy(d, z).wait_send()))
    rim_up = copy(og_ref, ogr.at[0], rim_s.at[0], rim_r.at[0], f, (s + 1) % 16)
    rim_down = copy(og_ref, ogr.at[1], rim_s.at[1], rim_r.at[1], f, (s + 15) % 16)
    start(rim_up)
    start(rim_down)
    loop(1, 32, lambda d: zw_copy(d, (z - d + NZ) % NZ).wait_recv())

    slot = lax.broadcasted_iota(jnp.int32, (160, 256), 1)
    row = lax.broadcasted_iota(jnp.int32, (160, 256), 0)
    pick = jnp.where(((slot >> 3) * 5 + (slot & 7) == row) & ((slot & 7) < 5), 1.0, 0.0).astype(BF16)
    pieces = zbuf[...].astype(F32).reshape(256, BLK).astype(BF16)
    wbuf[pl.ds(pl.multiple_of(yh * 160, 32), 160), pl.ds(mycol, BLK)] = nn(pick, pieces).astype(BF16)

    def to_sibling(i, j):
        ref = wblock(*second_block(i, j, c), c)
        n = 4 * j + i
        return copy(ref, ref, p3_s.at[n], p3_r.at[n], f, sib)

    def onward(i, j):
        ref = wblock(*first_block(i), c)
        n = 4 * j + i
        fd, sd = on_chip(((y + (1 - c) * j) % 4) * 4 + (x + c * j) % 4, c)
        return copy(ref, ref, p2_s.at[n], p2_r.at[n], fd, sd)

    def first_block(i):
        return (y - c * i + 4) % 4, (x - (1 - c) * i + 4) % 4

    def second_block(i, j, cc):
        return (y - (1 - cc) * j - cc * i + 8) % 4, (x - cc * j - (1 - cc) * i + 8) % 4

    mine = wblock(y, x, c)
    for j in range(1, 4):
        fd, sd = on_chip(((y + c * j) % 4) * 4 + (x + (1 - c) * j) % 4, c)
        start(copy(mine, mine, p1_s.at[j], p1_r.at[j], fd, sd))
    def forward(i):
        for j in range(1, 4):
            onward(i, j).start()
        to_sibling(i, 0).start()

    for i in range(4):
        if i:
            ref = wblock(*first_block(i), c)
            copy(ref, ref, p1_s.at[i], p1_r.at[i], f, sib).wait_recv()
        pl.when(first_block(i)[1] < 3)(lambda i=i: forward(i))

    def second(i, j):
        ref = wblock(*second_block(i, j, c), c)
        n = 4 * j + i
        copy(ref, ref, p2_s.at[n], p2_r.at[n], f, sib).wait_recv()
        to_sibling(i, j).start()

    def from_sibling(i, j):
        ref = wblock(*second_block(i, j, 1 - c), 1 - c)
        n = 4 * j + i
        copy(ref, ref, p3_s.at[n], p3_r.at[n], f, sib).wait_recv()

    def wanted(bx, temporal):
        return bx == 3 if temporal else bx < 3

    def take_own(temporal):
        for i in range(4):
            for j in range(1, 4):
                pl.when(wanted(second_block(i, j, c)[1], temporal))(lambda i=i, j=j: second(i, j))

    def take_sibling(temporal):
        for i in range(4):
            for j in range(4):
                pl.when(wanted(second_block(i, j, 1 - c)[1], temporal))(lambda i=i, j=j: from_sibling(i, j))

    def blocks_gone():
        for i in range(4):
            for j in range(4):
                if j:
                    onward(i, j).wait_send()
                to_sibling(i, j).wait_send()

    pending.append(blocks_gone)
    take_own(False)
    for i in range(4):
        pl.when(first_block(i)[1] == 3)(lambda i=i: forward(i))

    def lane_sums(values):
        part = values[:, 0:128] + values[:, 128:256] + values[:, 256:384]
        return jnp.sum(part.T, axis=0, keepdims=True)

    def sums_of(first, second):
        return jnp.concatenate([lane_sums(first), lane_sums(second)], axis=0)

    def exchange(buf, value, send, recv):
        buf[s] = value

        def go(j):
            return copy(buf.at[s], buf.at[s], send.at[j], recv.at[j], f, (s + j) % 16)

        loop(1, 16, lambda j: go(j).start())
        pending.append(lambda: loop(1, 16, lambda j: go(j).wait_send()))

    def arrived(buf, send, recv):
        def take(j):
            src = (s - j + 16) % 16
            copy(buf.at[src], buf.at[src], send.at[j], recv.at[j], f, src).wait_recv()

        loop(1, 16, take)

    def columns_of(cc):
        cols = pl.ds(pl.multiple_of(cc * (TIME_AT // 2), BLK), TIME_AT // 2)
        return nn(wbuf[:, cols], xcol[cols, :])

    hidden = columns_of(c)
    take_sibling(False)
    hidden = hidden + columns_of(1 - c)
    exchange(st1, sums_of(hidden, hidden * hidden), st1_s, st1_r)
    wtrans[...] = wbuf[:, 0:TIME_AT].T

    has_left = jnp.where(s > 0, 1.0, 0.0)
    has_right = jnp.where(s < FRAMES - 1, 1.0, 0.0)
    rim_up.wait_recv()
    rim_down.wait_recv()
    per = CH // GROUPS
    row_i = lax.broadcasted_iota(jnp.int32, (CH, CH), 0)
    col_i = lax.broadcasted_iota(jnp.int32, (CH, CH), 1)
    low = row_i - (row_i % per)
    same = jnp.where((col_i >= low) & (col_i < low + per), 1.0, 0.0)
    counted = float(FRAMES * PIXELS * per)

    def group_means(buf):
        grouped = lax.dot_general(
            same,
            jnp.sum(buf[...], axis=0),
            (((1,), (1,)), ((), ())),
            precision=lax.Precision.HIGHEST,
            preferred_element_type=F32,
        )
        return grouped[:, 0:1] / counted, grouped[:, 1:2] / counted

    def column(ref):
        return jnp.broadcast_to(ref[...].reshape(1, CH), (8, CH)).T[:, 0:1]

    gain = column(gain_ref)
    shift = column(shift_ref)

    arrived(st1, st1_s, st1_r)
    average, squares = group_means(st1)
    inv_std = lax.rsqrt(squares - average * average + EPSILON)
    normed = (hidden - average) * inv_std
    preact = normed * gain + shift
    sig = 1.0 / (1.0 + jnp.exp(-preact))
    activation = (preact * sig).astype(BF16)
    act_ref[...] = activation

    def share_of(part):
        pieces = []
        for k, weight in enumerate((has_right, None, has_left)):
            ref = (ogr.at[1], og_ref, ogr.at[0])[k]
            rows = jnp.concatenate(
                [ref[pl.ds(pl.multiple_of(160 * h + 80 * part, 16), 80), :] for h in range(2)], axis=0
            )
            piece = nt(rows, activation)
            pieces.append(piece if weight is None else piece * weight)
        pieces.append(jnp.zeros((160, 64), F32))
        return jnp.concatenate(pieces, axis=1).reshape(2, 80, 1024)

    gout[...] = share_of(1 - c).astype(BF16)
    core_copy = copy(gout, gsib, gc_s.at[0], gc_r.at[0], f, sib)
    start(core_copy)
    own_share = share_of(c)

    core_copy.wait_recv()
    gchip[...] = (own_share + gsib[...].astype(F32)).astype(BF16)

    def tile_of(q):
        return gchip.at[q // 8, :, pl.ds(pl.multiple_of((q % 8) * 128, 128), 128)]

    def plane_step(j):
        return ((y + j // 4) % 4) * 4 + (x + j % 4) % 4

    def gp_copy(j, to, src):
        fd, sd = on_chip(to, c)
        return copy(tile_of(to), gplane.at[src], gp_s.at[j], gp_r.at[j], fd, sd)

    for j in sorted(range(1, 16), key=lambda j: -min(j // 4, 4 - j // 4) - min(j % 4, 4 - j % 4)):
        gp_copy(j, plane_step(j), chip).start()
    pending.append(lambda: loop(1, 16, lambda j: gp_copy(j, plane_step(j), chip).wait_send()))
    gplane[chip] = gchip[chip // 8, :, pl.ds(pl.multiple_of((chip % 8) * 128, 128), 128)]

    take_own(True)
    take_sibling(True)
    wtime = wbuf[:, TIME_AT:COLS]
    taps = [wtime[:, k * CH : (k + 1) * CH] for k in range(3)]
    act_grad = (
        (
            nn(taps[0].T, ogr[1]) * has_right
            + nn(taps[1].T, og_ref[...])
            + nn(taps[2].T, ogr[0]) * has_left
        )
        .astype(BF16)
        .astype(F32)
    )
    scaled = act_grad * (sig * (1.0 + preact * (1.0 - sig))) * gain
    exchange(st2, sums_of(scaled, scaled * normed), st2_s, st2_r)

    def gp_take(j):
        src = plane_step(16 + 4 * ((4 - j // 4) % 4) + (4 - j % 4) % 4)
        gp_copy(j, src, src).wait_recv()

    loop(1, 16, gp_take)
    share = jnp.zeros((80, 128), F32)
    for i in range(16):
        share = share + gplane[i].astype(F32)

    slot = lax.broadcasted_iota(jnp.int32, (128, 80), 0)
    row = lax.broadcasted_iota(jnp.int32, (128, 80), 1)
    put = jnp.where(((slot >> 3) * 5 + (slot & 7) == row) & ((slot & 7) < 5), 1.0, 0.0).astype(BF16)
    zsend[...] = nn(put, share.astype(BF16)).reshape(16, 8, 128).astype(BF16)
    owner = z // 16 == c

    def gz_copy(d):
        return copy(zsend.at[(z + d) % 16], zrecv.at[d], gz_s.at[d], gz_r.at[d], zpeer(d), s)

    def to_owner(d, act):
        @pl.when(((z + d) % NZ) // 16 == c)
        def _():
            act(gz_copy(d))

    loop(0, 31, lambda i: to_owner(flight_order(i), lambda cp: cp.start()))
    pending.append(lambda: loop(1, 32, lambda d: to_owner(d, lambda cp: cp.wait_send())))

    arim_up = copy(act_ref, actr.at[0], arim_s.at[0], arim_r.at[0], f, (s + 1) % 16)
    arim_down = copy(act_ref, actr.at[1], arim_s.at[1], arim_r.at[1], f, (s + 15) % 16)
    start(arim_up)
    start(arim_down)

    arrived(st2, st2_s, st2_r)
    mean_one, mean_two = group_means(st2)
    hid_grad = (inv_std * (scaled - mean_one - normed * mean_two)).astype(BF16)

    total = nn(wtrans[4 * CH : 5 * CH, :], hid_grad)
    for a in range(3):
        for b in range(3):
            if a != 1 or b != 1:
                at = (3 * a + b) * CH
                total = total + moved(nn(wtrans[at : at + CH, :], hid_grad), 2 - a, 2 - b)
    ing_ref[...] = total.astype(BF16)
    ing_out = pltpu.make_async_copy(ing_ref, ing_hbm, out_sem.at[0])
    ing_out.start()
    arim_up.wait_recv()
    arim_down.wait_recv()
    mixed_ref[...] = (
        nn(taps[0], actr[0]) * has_left + nn(taps[1], act_ref[...]) + nn(taps[2], actr[1]) * has_right
    ).astype(BF16)

    mixed_out = pltpu.make_async_copy(mixed_ref, mixed_hbm, out_sem.at[1])
    mixed_out.start()

    for left_over in pending:
        left_over()

    def fin_copy(j, src):
        return copy(fval, fin.at[src], fin_s.at[j], fin_r.at[src], f, (s + j) % 16)

    @pl.when(owner)
    def _():
        zrecv[0] = zsend[z % 16]
        loop(1, 32, lambda d: gz_copy(d).wait_recv())
        last = jnp.sum(zrecv[...].astype(F32), axis=0) * (1.0 / (lax.axis_size("fsdp") * FRAMES))
        fval[...] = last
        loop(1, 16, lambda j: fin_copy(j, chip % 8).start())
        fin[chip % 8] = last

    def fin_take(src):
        @pl.when(jnp.logical_not(owner) | (src != chip % 8))
        def _():
            fin_copy(1, src).wait_recv()

    loop(0, 8, fin_take)
    gt_ref[...] = jnp.concatenate([fin[t] for t in range(8)], axis=1)[0:5, 0 : 3 * CH]
    gt_out = pltpu.make_async_copy(gt_ref, gt_hbm, out_sem.at[2])
    gt_out.start()

    @pl.when(owner)
    def _():
        loop(1, 16, lambda j: fin_copy(j, chip % 8).wait_send())

    ing_out.wait()
    mixed_out.wait()
    gt_out.wait()


def local(clips_in, weight_space, weight_time, norm_gain, norm_shift, out_grad):
    dma = pltpu.SemaphoreType.DMA
    hbm = pl.BlockSpec(memory_space=pltpu.HBM)
    anywhere = pl.BlockSpec(memory_space=pl.ANY)
    mixed, in_grad, grad_time = pl.pallas_call(
        kernel,
        out_shape=(
            jax.ShapeDtypeStruct((CH, PIXELS), BF16),
            jax.ShapeDtypeStruct((CH, PIXELS), BF16),
            jax.ShapeDtypeStruct((5, 3 * CH), F32),
        ),
        in_specs=[hbm] * 6,
        out_specs=(anywhere, anywhere, anywhere),
        scratch_shapes=[
            pltpu.VMEM((CH, PIXELS), BF16),
            pltpu.VMEM((5, 9 * CH), BF16),
            pltpu.VMEM((5, 3 * CH), BF16),
            pltpu.VMEM((CH,), F32),
            pltpu.VMEM((CH,), F32),
            pltpu.VMEM((CH, PIXELS), BF16),
            pltpu.VMEM((CH, PIXELS), BF16),
            pltpu.VMEM((CH, PIXELS), BF16),
            pltpu.VMEM((5, 3 * CH), F32),
            pltpu.VMEM((2, CH, PIXELS), BF16),
            pltpu.VMEM((8, COLS), F32),
            pltpu.VMEM((NZ, 8, BLK), BF16),
            pltpu.VMEM((CH, COLS), BF16),
            pltpu.VMEM((TIME_AT, PIXELS), BF16),
            pltpu.VMEM((16, 2, CH), F32),
            pltpu.VMEM((16, 2, CH), F32),
            pltpu.VMEM((CH, PIXELS), BF16),
            pltpu.VMEM((2, CH, PIXELS), BF16),
            pltpu.VMEM((2, 80, 1024), BF16),
            pltpu.VMEM((2, 80, 1024), BF16),
            pltpu.VMEM((2, 80, 1024), BF16),
            pltpu.VMEM((16, 80, 128), BF16),
            pltpu.VMEM((16, 8, 128), BF16),
            pltpu.VMEM((NZ, 8, 128), BF16),
            pltpu.VMEM((8, 128), F32),
            pltpu.VMEM((8, 8, 128), F32),
            pltpu.VMEM((TIME_AT, CH), BF16),
        ]
        + [dma((n,)) for n in (2, 2, NZ, NZ, 4, 4)]
        + [dma((16,))] * 8
        + [dma((2,))] * 2
        + [dma((1,))] * 2
        + [dma((16,))] * 2
        + [dma((NZ,))] * 2
        + [dma((16,)), dma((8,)), dma((6,)), dma((3,))],
        compiler_params=pltpu.CompilerParams(
            collective_id=0, has_side_effects=True, vmem_limit_bytes=24 * 1024 * 1024
        ),
    )(
        *(
            pltpu.with_memory_space_constraint(v, pltpu.HBM)
            for v in (
                clips_in.reshape(PIXELS, CH).T,
                weight_space,
                weight_time,
                norm_gain,
                norm_shift,
                out_grad.reshape(PIXELS, CH).T,
            )
        )
    )
    return mixed.T.reshape(clips_in.shape), in_grad.T.reshape(clips_in.shape), grad_time


def solution(mesh):
    in_specs = (
        P("fsdp", "seq", None, None),
        P("fsdp", None),
        P("fsdp", None),
        P(),
        P(),
        P("fsdp", "seq", None, None),
    )
    out_specs = (P("fsdp", "seq", None, None), P("fsdp", "seq", None, None), P("fsdp", None))
    return jax.shard_map(local, mesh=mesh, in_specs=in_specs, out_specs=out_specs, check_vma=False)
```
